128 devices in a mesh: sample: 8 (over z_lo, x), depth: 16 (over z_hi, y, core).
Axes of the slice: x: 4, y: 4, z: 4 (z_hi: 2, z_lo: 2; z = z_hi * 2 + z_lo), core: 2. Of those that a mesh axis runs over, the one named last changes fastest.
Arguments:
- volume: bfloat16 [8, 16, 32, 2048], P('sample', 'depth'), may hold values from -6 to 6
- conv1_weight: bfloat16 [27, 64, 64], replicated, may hold values from -0.15625 to 0.15625
- conv2_weight: bfloat16 [27, 1024, 1024], P(None, 'depth'), may hold values from -0.0390625 to 0.0390625
- cotangent: bfloat16 [8, 16, 8, 8, 1024], P('sample', 'depth'), may hold values from -6 to 6
Outputs:
- features_out: bfloat16 [8, 16, 8, 8, 1024], P('sample', 'depth')
- grad_volume: bfloat16 [8, 16, 32, 2048], P('sample', 'depth')
- grad_conv1: float32 [27, 64, 64], replicated
- grad_conv2: float32 [27, 1024, 1024], P(None, 'depth')
The draws below stay inside these ranges and needn't reach their ends.
All inputs are finite; a program needn't handle non-finite values.
Results may differ from the reference program's by a relative error of at most 0.014.
Values may be sent and summed in bfloat16 or wider, within the bound.
A program may use at most 256 MiB of HBM per device.

```python
import math
import jax
import jax.numpy as jnp
from jax import lax

C1 = 64
LAT = 32
BLOCK = 4
C2 = 1024
LS = 8
DEPTH = 16
SAMPLES = 8


def block_levels(rng, extent, cuts, least, high):
    def one(position, blocks):
        steps = jax.random.uniform(jax.random.fold_in(jax.random.fold_in(rng, 6), position), (blocks,), jnp.float32, least / len(cuts), high / len(cuts))
        return jnp.repeat(jnp.exp(steps), extent[position] // blocks).reshape((-1,) + (1,) * (len(extent) - position - 1))

    gain = one(*cuts[0])
    for cut in cuts[1:]:
        gain = gain * one(*cut)
    return gain


def normal_values(own_key, extent, scale, bound, shards=(), dtype=jnp.bfloat16):
    entries = jax.random.normal(own_key, extent, jnp.float32) * scale
    if len(shards) > 0:
        entries = block_levels(own_key, extent, shards, -0.22, 0.18) * entries
    return jnp.clip(entries, min=-bound, max=bound).astype(dtype)


def setup_inputs(seed: int = 0) -> dict:
    keys = jax.random.split(jax.random.key(seed), 5)
    volume = normal_values(keys[0], (SAMPLES, DEPTH, LAT, LAT * C1), 1.0, 6.0, ((0, 8), (1, 16)))
    conv1_weight = normal_values(keys[1], (27, C1, C1), (27 * C1) ** -0.5, 0.15625)
    conv2_weight = normal_values(keys[2], (27, C2, C2), (27 * C2) ** -0.5, 0.0390625, ((1, 16),))
    cotangent = normal_values(keys[3], (SAMPLES, DEPTH, LS, LS, C2), 1.0, 6.0, ((0, 8), (1, 16)))
    return dict(volume=volume, conv1_weight=conv1_weight, conv2_weight=conv2_weight, cotangent=cotangent)


root_coef = 0.7978845608028654
cubic_coef = 0.044715

def gelu_tanh(value):
    inner = root_coef * (value + cubic_coef * value * value * value)
    return 0.5 * value * (1.0 + jnp.tanh(inner))

def gelu_slope(value):
    inner = root_coef * (value + cubic_coef * value * value * value)
    tanh_val = jnp.tanh(inner)
    return 0.5 * (1.0 + tanh_val) + 0.5 * value * (1.0 - tanh_val * tanh_val) * root_coef * (1.0 + 3.0 * cubic_coef * value * value)

def patches(padded, planes):
    rows = padded.shape[1] - 2
    columns = padded.shape[2] - 2
    pieces = [padded[a:a + planes, b:b + rows, c:c + columns, :] for a in range(3) for b in range(3) for c in range(3)]
    return jnp.concatenate(pieces, axis=3).reshape(planes * rows * columns, -1)

def pad_all(field):
    return jnp.pad(field, ((1, 1), (1, 1), (1, 1), (0, 0)))

def adjoint_weight(weight, chans_in, chans_out):
    shaped = weight.reshape(3, 3, 3, chans_in, chans_out)[::-1, ::-1, ::-1]
    return jnp.swapaxes(shaped, 3, 4).reshape(27 * chans_out, chans_in)

def reference(volume, conv1_weight, conv2_weight, cotangent):
    flat_one = conv1_weight.reshape(27 * C1, C1)
    flat_two = conv2_weight.reshape(27 * C2, C2)
    back_one = adjoint_weight(conv1_weight, C1, C1)
    back_two = adjoint_weight(conv2_weight, C2, C2)

    def one_sample(carry, inputs):
        acc_one, acc_two = carry
        sample_vol, sample_cot = inputs
        field = sample_vol.reshape(DEPTH, LAT, LAT, C1)
        taps_one = patches(pad_all(field), DEPTH)
        pre = jnp.dot(taps_one, flat_one, preferred_element_type=jnp.float32)
        hidden = gelu_tanh(pre).astype(jnp.bfloat16)
        moved = hidden.reshape(DEPTH, LS, BLOCK, LS, BLOCK, C1).transpose(0, 1, 3, 2, 4, 5).reshape(DEPTH, LS, LS, C2)
        taps_two = patches(pad_all(moved), DEPTH)
        output = jnp.dot(taps_two, flat_two, preferred_element_type=jnp.float32).astype(jnp.bfloat16)
        output = output.reshape(DEPTH, LS, LS, C2)
        cot_flat = sample_cot.reshape(DEPTH * LS * LS, C2)
        acc_two = acc_two + jnp.dot(taps_two.T, cot_flat, preferred_element_type=jnp.float32)
        grad_moved = jnp.dot(patches(pad_all(sample_cot), DEPTH), back_two, preferred_element_type=jnp.float32).astype(jnp.bfloat16)
        spread = grad_moved.reshape(DEPTH, LS, LS, BLOCK, BLOCK, C1).transpose(0, 1, 3, 2, 4, 5).reshape(DEPTH * LAT * LAT, C1)
        grad_pre = (spread.astype(jnp.float32) * gelu_slope(pre)).astype(jnp.bfloat16)
        acc_one = acc_one + jnp.dot(taps_one.T, grad_pre, preferred_element_type=jnp.float32)
        grad_field = grad_pre.reshape(DEPTH, LAT, LAT, C1)
        grad_in = jnp.dot(patches(pad_all(grad_field), DEPTH), back_one, preferred_element_type=jnp.float32).astype(jnp.bfloat16)
        return ((acc_one, acc_two), (output, grad_in.reshape(DEPTH, LAT, LAT * C1)))
    start = (jnp.zeros((27 * C1, C1), jnp.float32), jnp.zeros((27 * C2, C2), jnp.float32))
    (acc_one, acc_two), (features_out, grad_volume) = lax.scan(one_sample, start, (volume, cotangent))
    scale_one = 1.0 / math.sqrt(SAMPLES * DEPTH * LAT * LAT)
    scale_two = 1.0 / math.sqrt(SAMPLES * DEPTH * LS * LS)
    grad_conv1 = (acc_one * scale_one).reshape(27, C1, C1)
    grad_conv2 = (acc_two * scale_two).reshape(27, C2, C2)
    return (features_out, grad_volume, grad_conv1, grad_conv2)
```

```python
import functools
import math

import jax
import jax.numpy as jnp
from jax import lax
from jax.experimental import pallas as pl
from jax.experimental.pallas import tpu as pltpu
from jax.sharding import PartitionSpec as P

MESH = pl.DeviceIdType.MESH
F32 = jnp.float32
BF16 = jnp.bfloat16
ROOT = 0.7978845608028654
CUBIC = 0.044715
SCALE1 = 1.0 / math.sqrt(8 * 16 * 32 * 32)
SCALE2 = 1.0 / math.sqrt(8 * 16 * 8 * 8)
VM = pl.BlockSpec(memory_space=pltpu.VMEM)
ANY = pl.BlockSpec(memory_space=pl.ANY)
LIMIT = 60 * 1024 * 1024


def where_am_i():
    s = lax.axis_index("sample")
    d = lax.axis_index("depth")
    return s, d


def rcopy(src, dst, ss, rs, dev):
    return pltpu.make_async_remote_copy(
        src_ref=src, dst_ref=dst, send_sem=ss, recv_sem=rs, device_id=dev, device_id_type=MESH
    )


def depth_peer(d, jz, jy, jc):
    zh, y, c = d // 8, (d // 2) % 4, d % 2
    return ((zh + jz) % 2) * 8 + ((y + jy) % 4) * 2 + (c + jc) % 2


def depth_src(d, jz, jy, jc):
    zh, y, c = d // 8, (d // 2) % 4, d % 2
    return ((zh + jz) % 2) * 8 + ((y + 4 - jy) % 4) * 2 + (c + jc) % 2


def sample_peer(s, jz, jx):
    return ((s // 4 + jz) % 2) * 4 + (s % 4 + jx) % 4


def sample_src(s, jz, jx):
    return ((s // 4 + jz) % 2) * 4 + (s % 4 + 4 - jx) % 4


CHIPS = [(jz, jy) for jz in range(2) for jy in range(4) if (jz, jy) != (0, 0)]
SAMPS = [(jz, jx) for jz in range(2) for jx in range(4) if (jz, jx) != (0, 0)]


def barrier(devs):
    bar = pltpu.get_barrier_semaphore()
    for dev in devs:
        pl.semaphore_signal(bar, inc=1, device_id=dev, device_id_type=MESH)
    pl.semaphore_wait(bar, len(devs))


def onehot(shape, fn):
    row = lax.broadcasted_iota(jnp.int32, shape, 0)
    col = lax.broadcasted_iota(jnp.int32, shape, 1)
    return jnp.where(fn(row, col), 1.0, 0.0).astype(BF16)


def dot(a, b):
    return jnp.dot(a, b, preferred_element_type=F32)


def nat(rho):
    return 4 * (rho % 8) + rho // 8


def call(kern, outs, ins, scratch, name, cid=None, specs=None, out_specs=None, **kw):
    params = dict(vmem_limit_bytes=LIMIT)
    if cid is not None:
        params.update(collective_id=cid, has_side_effects=True)
    return pl.pallas_call(
        kern,
        out_shape=outs,
        in_specs=specs or [VM] * len(ins),
        out_specs=out_specs or [VM] * len(outs),
        scratch_shapes=scratch,
        compiler_params=pltpu.CompilerParams(**params),
        name=name,
    )(*ins)


def sds(shape, dtype=BF16):
    return jax.ShapeDtypeStruct(shape, dtype)


def c1_kernel(v, cot, w, vp, vn, call_, csl, woth, cotp, mine, hs, hr, gs, gr, fs, fr, as_, ar, g2s, g2r, f2s, f2r, ws, wr):
    s, d = where_am_i()
    up, down = (d + 1) % 16, (d + 15) % 16
    partner = depth_peer(d, 0, 0, 1)
    barrier(
        [(s, up), (s, down), (s, partner)]
        + [(s, depth_peer(d, jz, jy, 0)) for jz, jy in CHIPS]
        + [(sample_peer(s, jz, jx), d) for jz, jx in SAMPS]
    )
    halo = [
        rcopy(v, vp, hs.at[0], hr.at[0], (s, up)),
        rcopy(v, vn, hs.at[1], hr.at[1], (s, down)),
    ]
    for h in halo:
        h.start()
    wx = rcopy(w, woth, ws, wr, (s, partner))
    wx.start()
    perm = onehot((64, 64), lambda u, q: q == (u % 8) * 8 + u // 8)
    cotp[...] = dot(perm, cot[...]).astype(BF16)
    a2a = []
    for i, (jz, jx) in enumerate(SAMPS):
        t = sample_peer(s, jz, jx)
        a2a.append(rcopy(cotp.at[:, pl.ds(t * 128, 128)], mine.at[s], as_.at[i], ar.at[i], (t, d)))
        a2a[-1].start()
    first = [rcopy(cotp, call_.at[d], gs.at[i], gr.at[i], (s, depth_peer(d, jz, jy, 0))) for i, (jz, jy) in enumerate(CHIPS)]
    first.append(rcopy(cotp, call_.at[d], gs.at[7], gr.at[7], (s, partner)))
    for f in first:
        f.start()
    mine[s] = cotp[:, pl.ds(s * 128, 128)]
    call_[d] = cotp[...]
    for i, (jz, jx) in enumerate(SAMPS):
        t = sample_src(s, jz, jx)
        rcopy(mine.at[t], mine.at[t], as_.at[i], ar.at[i], (t, d)).wait_recv()
    second = [rcopy(mine, csl.at[d], g2s.at[i], g2r.at[i], (s, depth_peer(d, jz, jy, 0))) for i, (jz, jy) in enumerate(CHIPS)]
    second.append(rcopy(mine, csl.at[d], g2s.at[7], g2r.at[7], (s, partner)))
    for f in second:
        f.start()
    csl[d] = mine[...]
    fwd = []
    for buf, sems in ((call_, (gs, gr, fs, fr)), (csl, (g2s, g2r, f2s, f2r))):
        for i, (jz, jy) in enumerate(CHIPS):
            q = depth_src(d, jz, jy, 0)
            rcopy(buf.at[q], buf.at[q], sems[0].at[i], sems[1].at[i], (s, q)).wait_recv()
            f = rcopy(buf.at[q], buf.at[q], sems[2].at[i], sems[3].at[i], (s, partner))
            f.start()
            fwd.append(f)
    for buf, sems in ((call_, (gs, gr, fs, fr)), (csl, (g2s, g2r, f2s, f2r))):
        rcopy(buf.at[partner], buf.at[partner], sems[0].at[7], sems[1].at[7], (s, partner)).wait_recv()
        for i, (jz, jy) in enumerate(CHIPS):
            q = depth_src(d, jz, jy, 1)
            rcopy(buf.at[q], buf.at[q], sems[2].at[i], sems[3].at[i], (s, partner)).wait_recv()
    for h in halo:
        h.wait()
    wx.wait()
    for f in a2a + first + second + fwd:
        f.wait_send()


def c1(v, cot, w):
    dma = pltpu.SemaphoreType.DMA
    return call(
        c1_kernel,
        [sds((32, 2048)), sds((32, 2048)), sds((16, 64, 1024)), sds((16, 8, 64, 128)), sds((27, 64, 1024))],
        [v, cot, w],
        [pltpu.VMEM((64, 1024), BF16), pltpu.VMEM((8, 64, 128), BF16)]
        + [dma((2,)), dma((2,)), dma((8,)), dma((8,)), dma((7,)), dma((7,)), dma((7,)), dma((7,))]
        + [dma((8,)), dma((8,)), dma((7,)), dma((7,)), dma(()), dma(())],
        "exchange_in",
        cid=1,
        specs=[VM, VM, ANY],
        out_specs=[VM, VM, VM, VM, ANY],
    )


def fill_band(band, dd):
    band[...] = jnp.zeros_like(band)
    for ab in range(9):
        band[pl.ds(ab * 512 + 64, 256), 0:128] = dd[ab]
        band[pl.ds(ab * 512 + 192, 256), 128:256] = dd[ab]


def fill_rows(lhs, planes, perms):
    zero = jnp.zeros((32, 128), BF16)
    for a in range(3):
        for b in range(3):
            x = planes[a] if perms[b] is None else dot(perms[b], planes[a]).astype(BF16)
            xp = jnp.concatenate([zero, x, zero], axis=1)
            for j in range(8):
                lhs[pl.ds(j * 32, 32), pl.ds((3 * a + b) * 512, 512)] = xp[:, 256 * j : 256 * j + 512]


def edge_planes(prev, own, nxt, d):
    zero = jnp.zeros_like(own)
    return [jnp.where(d > 0, prev, zero), own, jnp.where(d < 15, nxt, zero)]


def gelu_parts(value):
    inner = ROOT * (value + CUBIC * value * value * value)
    return jnp.tanh(inner)


def k2_kernel(vp, v, vn, dd, pre, moved, lhs, band):
    s, d = where_am_i()
    fill_band(band, dd)
    perms = [onehot((32, 32), lambda rho, i, b=b: i == nat(rho) + b - 1) for b in range(3)]
    fill_rows(lhs, edge_planes(vp[...], v[...], vn[...], d), perms)
    res = dot(lhs[...], band[...])
    for r in range(4):
        part = jnp.concatenate([res[j * 32 + r * 8 : j * 32 + r * 8 + 8] for j in range(8)], axis=0)
        pre[r] = part
        hid = (0.5 * part * (1.0 + gelu_parts(part))).astype(BF16)
        moved[2 * r] = hid[:, 0:128]
        moved[2 * r + 1] = hid[:, 128:256]


def k2(vp, v, vn, dd):
    return call(
        k2_kernel,
        [sds((4, 64, 256), F32), sds((8, 64, 128)), sds((256, 4608))],
        [vp, v, vn, dd],
        [pltpu.VMEM((4608, 256), BF16)],
        "conv1",
    )


def c3_kernel(moved, mk, as_, ar, gs, gr, fs, fr):
    s, d = where_am_i()
    c = d % 2
    partner = depth_peer(d, 0, 0, 1)
    offs = [(jz, jy, jc) for jz in range(2) for jy in range(4) for jc in range(2) if (jz, jy, jc) != (0, 0, 0)]
    barrier([(s, depth_peer(d, *o)) for o in offs] + [(sample_peer(s, *o), d) for o in SAMPS])
    a2a = []
    for i, o in enumerate(offs):
        t = depth_peer(d, *o)
        a2a.append(rcopy(moved.at[t // 2], mk.at[s, d], as_.at[i], ar.at[i], (s, t)))
        a2a[-1].start()
    mk[s, d] = moved[d // 2]
    for i, o in enumerate(offs):
        q = depth_src(d, *o)
        rcopy(mk.at[s, q], mk.at[s, q], as_.at[i], ar.at[i], (s, q)).wait_recv()
    half = pl.ds(c * 8, 8)
    other = pl.ds(8 - c * 8, 8)
    g = []
    for i, o in enumerate(SAMPS):
        g.append(rcopy(mk.at[s, half], mk.at[s, half], gs.at[i], gr.at[i], (sample_peer(s, *o), d)))
        g[-1].start()
    f = []
    for i, o in enumerate(SAMPS):
        t = sample_src(s, *o)
        rcopy(mk.at[t, half], mk.at[t, half], gs.at[i], gr.at[i], (t, d)).wait_recv()
        f.append(rcopy(mk.at[t, half], mk.at[t, half], fs.at[i], fr.at[i], (s, partner)))
        f[-1].start()
    for i, o in enumerate(SAMPS):
        t = sample_src(s, *o)
        rcopy(mk.at[t, other], mk.at[t, other], fs.at[i], fr.at[i], (s, partner)).wait_recv()
    for x in a2a + g + f:
        x.wait_send()


def c3(moved):
    dma = pltpu.SemaphoreType.DMA
    return call(
        c3_kernel,
        [sds((8, 16, 64, 128))],
        [moved],
        [dma((15,)), dma((15,)), dma((7,)), dma((7,)), dma((7,)), dma((7,))],
        "exchange_moved",
        cid=2,
    )[0]


def row_shift(x, b):
    if b == 1:
        return x
    rows = x.shape[0]
    lane = lax.broadcasted_iota(jnp.int32, x.shape, 0) % 8
    if b == 0:
        return jnp.where(lane == 0, 0.0, pltpu.roll(x, 1, 0))
    return jnp.where(lane == 7, 0.0, pltpu.roll(x, rows - 1, 0))


def col_shift(x, c):
    if c == 1:
        return x
    zero = jnp.zeros((x.shape[0], 8, x.shape[2]), x.dtype)
    if c == 0:
        return jnp.concatenate([zero, x[:, :56]], axis=1)
    return jnp.concatenate([x[:, 8:], zero], axis=1)


def build_taps(x, s2):
    flat = x.astype(F32).reshape(1024, 128)
    for b in range(3):
        y = row_shift(flat, b).reshape(16, 64, 128)
        for c in range(3):
            s2[1:17, :, (3 * b + c) * 128 : (3 * b + c + 1) * 128] = col_shift(y, c).astype(BF16)


def k4_kernel(mk, call_, csl, w, woth, part, gm, piece, wv, s2, acc, wacc, sem):
    s, d = where_am_i()
    c = d % 2
    cps = [
        pltpu.make_async_copy(w, wv.at[:, c], sem.at[0]),
        pltpu.make_async_copy(woth, wv.at[:, 1 - c], sem.at[1]),
    ]
    for x in cps:
        x.start()
    s2[0] = jnp.zeros((64, 1152), BF16)
    s2[17] = jnp.zeros((64, 1152), BF16)
    build_taps(mk[s], s2)
    for x in cps:
        x.wait()

    def fwd(i, _):
        tot = jnp.zeros((256, 512), F32)
        for a in range(3):
            lhs = s2[pl.ds(4 * i + a, 4)].reshape(256, 1152)
            rhs = wv[9 * a : 9 * a + 9, :, :, pl.ds(pl.multiple_of(c * 512, 512), 512)].reshape(1152, 512)
            tot = tot + dot(lhs, rhs)
        part[pl.ds(4 * i, 4)] = tot.astype(BF16).reshape(4, 64, 512)
        return 0

    lax.fori_loop(0, 4, fwd, 0)

    def back(bc, _):
        tot = jnp.zeros((512, 128), F32)
        for a in range(3):
            q0 = 8 * c + 1 - a
            rows = []
            for i in range(8):
                q = q0 + i
                if i in (0, 7):
                    blk = call_[jnp.clip(q, 0, 15)]
                    blk = jnp.where((q >= 0) & (q < 16), blk, jnp.zeros_like(blk))
                else:
                    blk = call_[q]
                rows.append(blk)
            lhs = jnp.concatenate(rows, axis=0)
            rhs = wv[9 * a + bc].reshape(128, 1024)
            tot = tot + lax.dot_general(lhs, rhs, (((1,), (1,)), ((), ())), preferred_element_type=F32)
        acc[bc] = tot
        return 0

    lax.fori_loop(0, 9, back, 0)
    total = jnp.zeros((8, 64, 128), F32)
    for b in range(3):
        inner = jnp.zeros((8, 64, 128), F32)
        for cc in range(3):
            inner = inner + col_shift(acc[3 * b + cc].reshape(8, 64, 128), 2 - cc)
        total = total + row_shift(inner.reshape(512, 128), 2 - b).reshape(8, 64, 128)
    gm[...] = total.astype(BF16)

    wacc[...] = jnp.zeros_like(wacc)

    def wgrad(i, _):
        t = (s + i) % 8

        @pl.when(i > 0)
        def _():
            build_taps(mk[t], s2)

        ct = jnp.transpose(csl[:, t].reshape(1024, 128).astype(F32)).astype(BF16)
        wacc[:, 0:1152] += dot(ct, s2[pl.ds(2 * c, 16)].reshape(1024, 1152))
        wacc[:, 1152:1792] += dot(ct, s2[1:17, :, pl.ds(pl.multiple_of(c * 512, 512), 640)].reshape(1024, 640))
        return 0

    lax.fori_loop(0, 8, wgrad, 0)
    for i in range(14):
        piece[i] = jnp.transpose(wacc[:, i * 128 : i * 128 + 128] * SCALE2).astype(BF16)


def k4(mk, call_, csl, w, woth):
    return call(
        k4_kernel,
        [sds((16, 64, 512)), sds((8, 64, 128)), sds((14, 128, 128))],
        [mk, call_, csl, w, woth],
        [
            pltpu.VMEM((27, 2, 64, 1024), BF16),
            pltpu.VMEM((18, 64, 1152), BF16),
            pltpu.VMEM((9, 512, 128), F32),
            pltpu.VMEM((128, 1792), F32),
            pltpu.SemaphoreType.DMA((2,)),
        ],
        "conv2",
        specs=[VM, VM, VM, ANY, ANY],
    )


def c5_kernel(part, gm, piece, frecv, grecv, gw, rs_s, rs_r, g_s, g_r, p_s, p_r, n_s, n_r, h_s, h_r):
    s, d = where_am_i()
    c, m = d % 2, d // 2
    zl, x = s // 4, s % 4
    partner = depth_peer(d, 0, 0, 1)
    offs = [(jz, jy, jc) for jz in range(2) for jy in range(4) for jc in range(2) if (jz, jy, jc) != (0, 0, 0)]
    xp, xm, zo = sample_peer(s, 0, 1), sample_peer(s, 0, 3), sample_peer(s, 1, 0)
    barrier([(s, depth_peer(d, *o)) for o in offs] + [(xp, d), (xm, d), (zo, d)])
    mine = pl.ds(c * 14, 14)
    theirs = pl.ds(14 - c * 14, 14)
    px = rcopy(piece.at[:, pl.ds(64 - c * 64, 64)], gw.at[s, mine], p_s, p_r, (s, partner))
    px.start()
    gsend = []
    for i in range(8):
        p = 8 * c + i
        cp = rcopy(gm.at[i], grecv.at[m], g_s.at[i], g_r.at[m], (s, p))
        gsend.append((p, cp))

        @pl.when(p != d)
        def _(cp=cp):
            cp.start()

        @pl.when(p == d)
        def _(i=i):
            grecv[m] = gm[i]

    gw[s, mine] = piece[:, pl.ds(pl.multiple_of(c * 64, 64), 64)]
    rs = []
    for i, o in enumerate(offs):
        t = depth_peer(d, *o)
        rs.append(rcopy(part.at[t], frecv.at[m, c], rs_s.at[i], rs_r.at[i], (s, t)))
    rcopy(gw.at[s, theirs], gw.at[s, theirs], p_s, p_r, (s, partner)).wait_recv()
    half = (pl.ds(0, 14), pl.ds(14, 14))

    def send(k, block, dev, which=None):
        ref = gw.at[block] if which is None else gw.at[block, half[which]]
        cp = rcopy(ref, ref, n_s.at[k], n_r.at[k], (dev, d))
        cp.start()
        return cp

    def recv(k, block, which=None):
        ref = gw.at[block] if which is None else gw.at[block, half[which]]
        rcopy(ref, ref, n_s.at[k], n_r.at[k], (s, partner)).wait_recv()

    so = s % 4 + (1 - zl) * 4
    x2 = sample_peer(s, 0, 2)
    oxp, oxm, ox2 = sample_peer(so, 0, 1), sample_peer(so, 0, 3), sample_peer(so, 0, 2)
    sends = [send(0, s, zo), send(1, s, xp), send(2, s, xm)]
    for r in rs:
        r.start()
    frecv[m, c] = part[d]
    recv(1, xm)
    sends.append(send(3, xm, xp, 0))
    recv(2, xp)
    sends.append(send(4, xp, xm, 1))
    recv(0, so)
    sends.append(send(5, so, xp))
    sends.append(send(6, so, xm))
    recv(3, x2, 0)
    recv(4, x2, 1)
    recv(5, oxm)
    sends.append(send(7, oxm, xp, 0))
    recv(6, oxp)
    sends.append(send(8, oxp, xm, 1))
    for i, o in enumerate(offs):
        q = depth_src(d, *o)
        rcopy(frecv.at[q // 2, q % 2], frecv.at[q // 2, q % 2], rs_s.at[i], rs_r.at[i], (s, q)).wait_recv()
    for j in range(8):

        @pl.when((2 * j + d // 8) != d)
        def _(j=j):
            rcopy(grecv.at[j], grecv.at[j], g_s.at[0], g_r.at[j], (s, partner)).wait_recv()

    recv(7, ox2, 0)
    recv(8, ox2, 1)
    for p, cp in gsend:

        @pl.when(p != d)
        def _(cp=cp):
            cp.wait_send()

    px.wait_send()
    for r in rs + sends:
        r.wait_send()


def c5(part, gm, piece):
    dma = pltpu.SemaphoreType.DMA
    return call(
        c5_kernel,
        [sds((8, 2, 64, 512)), sds((8, 64, 128)), sds((8, 28, 64, 128))],
        [part, gm, piece],
        [dma((15,)), dma((15,)), dma((8,)), dma((8,)), dma(()), dma(()), dma((9,)), dma((9,)), dma(()), dma(())],
        "exchange_results",
        cid=3,
    )


def k6_kernel(frecv, grecv, pre, feat, gpn):
    tot = frecv[0].astype(F32)
    for i in range(1, 8):
        tot = tot + frecv[i].astype(F32)
    full = jnp.concatenate([tot[0], tot[1]], axis=1).astype(BF16)
    perm = onehot((64, 64), lambda u, q: q == (u % 8) * 8 + u // 8)
    feat[...] = dot(perm, full).astype(BF16)
    gp = []
    for r in range(4):
        z = pre[r]
        th = gelu_parts(z)
        slope = 0.5 * (1.0 + th) + 0.5 * z * (1.0 - th * th) * ROOT * (1.0 + 3.0 * CUBIC * z * z)
        spread = jnp.concatenate([grecv[2 * r], grecv[2 * r + 1]], axis=1).astype(F32)
        gp.append(spread * slope)
    for j in range(8):
        rows = jnp.concatenate([gp[r][8 * j : 8 * j + 8] for r in range(4)], axis=0)
        gpn[:, 256 * j : 256 * j + 256] = rows.astype(BF16)


def k6(frecv, grecv, pre):
    return call(k6_kernel, [sds((64, 1024)), sds((32, 2048))], [frecv, grecv, pre], [], "features_gradpre")


def c7_kernel(g, gp, gn, hs, hr):
    s, d = where_am_i()
    up, down = (d + 1) % 16, (d + 15) % 16
    barrier([(s, up), (s, down)])
    halo = [rcopy(g, gp, hs.at[0], hr.at[0], (s, up)), rcopy(g, gn, hs.at[1], hr.at[1], (s, down))]
    for h in halo:
        h.start()
    for h in halo:
        h.wait()


def c7(g):
    dma = pltpu.SemaphoreType.DMA
    return call(c7_kernel, [sds((32, 2048)), sds((32, 2048))], [g], [dma((2,)), dma((2,))], "halo_grad", cid=4)


def k8_kernel(gp, g, gn, lhs1, ddb, gvol, tsum, lhs, band):
    s, d = where_am_i()
    fill_band(band, ddb)
    perms = [onehot((32, 32), lambda u, q, b=b: nat(q) == nat(u) + b - 1) for b in range(3)]
    perms[1] = None
    fill_rows(lhs, edge_planes(gp[...], g[...], gn[...], d), perms)
    res = dot(lhs[...], band[...]).astype(BF16)
    wide = jnp.concatenate([res[32 * j : 32 * j + 32] for j in range(8)], axis=1)
    gvol[...] = dot(onehot((32, 32), lambda i, q: nat(q) == i), wide).astype(BF16)
    gx = jnp.concatenate([g[:, 256 * j : 256 * j + 256] for j in range(8)], axis=0)
    gt = jnp.transpose(gx.astype(F32)).astype(BF16)
    for ab in range(9):
        o = dot(gt, lhs1[:, 512 * ab : 512 * ab + 512])
        even = o[0:64, 0:256] + o[128:192, 128:384]
        t = o[64:128, 128:384] + o[192:256, 256:512] + pltpu.roll(even, 192, 1)
        tsum[64 * ab : 64 * ab + 64] = (t * SCALE1).astype(BF16)
    tsum[576:640] = jnp.zeros((64, 256), BF16)


def k8(gp, g, gn, lhs1, ddb):
    return call(
        k8_kernel,
        [sds((32, 2048)), sds((640, 256))],
        [gp, g, gn, lhs1, ddb],
        [pltpu.VMEM((256, 4608), BF16), pltpu.VMEM((4608, 256), BF16)],
        "conv1_back",
    )


def c9_kernel(t, out, pbuf, pbuf2, own, rbuf, rbuf2, dbuf, sem):
    s, d = where_am_i()
    c = d % 2
    partner = depth_peer(d, 0, 0, 1)
    barrier(
        [(s, partner)]
        + [(s, depth_peer(d, jz, jy, 0)) for jz, jy in CHIPS]
        + [(sample_peer(s, jz, jx), d) for jz, jx in SAMPS]
    )
    lane = pl.ds(pl.multiple_of(c * 128, 128), 128)
    lane2 = pl.ds(pl.multiple_of(128 - c * 128, 128), 128)
    cp = rcopy(t.at[:, lane2], pbuf, sem.at[0], sem.at[1], (s, partner))
    cp.start()
    cp.wait()
    own[...] = (t[:, lane].astype(F32) + pbuf[...].astype(F32)).astype(BF16)
    cps = []
    for i, o in enumerate(SAMPS):
        q = sample_peer(s, *o)
        cps.append(rcopy(own.at[pl.ds(pl.multiple_of(q * 80, 16), 80)], rbuf.at[i], sem.at[2 + i], sem.at[9 + i], (q, d)))
        cps[-1].start()
    mine = pl.ds(pl.multiple_of(s * 80, 16), 80)
    tot = own[mine].astype(F32)
    for i, x in enumerate(cps):
        x.wait()
        tot = tot + rbuf[i].astype(F32)
    dbuf[7] = tot.astype(BF16)
    cps = []
    for i, (jz, jy) in enumerate(CHIPS):
        cps.append(rcopy(dbuf.at[7], dbuf.at[i], sem.at[16 + i], sem.at[23 + i], (s, depth_peer(d, jz, jy, 0))))
        cps[-1].start()
    order = []
    for x in cps:
        x.wait()
    m = d // 2
    for j in range(8):
        order.append(j)
    tot = None
    for j in range(8):
        jz = ((j // 4) + (m // 4)) % 2
        jy = (m % 4 + 4 - j % 4) % 4
        idx = jz * 4 + jy
        idx = jnp.where(idx == 0, 7, idx - 1)
        val = dbuf[idx].astype(F32)
        tot = val if tot is None else tot + val
    own[mine] = tot.astype(BF16)
    cps = []
    for i, o in enumerate(SAMPS):
        q = sample_peer(s, *o)
        cps.append(rcopy(own.at[mine], rbuf2.at[i], sem.at[30 + i], sem.at[37 + i], (q, d)))
        cps[-1].start()
    for i, o in enumerate(SAMPS):
        cps[i].wait()
        q = sample_src(s, *o)
        own[pl.ds(pl.multiple_of(q * 80, 16), 80)] = rbuf2[i]
    cp = rcopy(own, pbuf2, sem.at[44], sem.at[45], (s, partner))
    cp.start()
    out[:, lane] = own[...]
    cp.wait()
    out[:, lane2] = pbuf2[...]


def c9(t):
    dma = pltpu.SemaphoreType.DMA
    return call(
        c9_kernel,
        [sds((640, 256))],
        [t],
        [
            pltpu.VMEM((640, 128), BF16),
            pltpu.VMEM((640, 128), BF16),
            pltpu.VMEM((640, 128), BF16),
            pltpu.VMEM((7, 80, 128), BF16),
            pltpu.VMEM((7, 80, 128), BF16),
            pltpu.VMEM((8, 80, 128), BF16),
            dma((46,)),
        ],
        "sum_conv1",
        cid=5,
    )[0]


def slot_of(t):
    return jnp.where(t < 14, t, jnp.where(t < 18, t + 10, t - 4))


def k10_kernel(gw, t, o2, o1):
    for q in range(8):
        o2[0, :, 128 * q : 128 * q + 128] = gw[q, 0].astype(F32)

    @pl.when(pl.program_id(0) == 0)
    def _():
        for ab in range(9):
            x = jnp.transpose(t[64 * ab : 64 * ab + 64].astype(F32))
            o1[3 * ab : 3 * ab + 3] = x[0:192].reshape(3, 64, 64)


def k10(gw, t):
    return pl.pallas_call(
        k10_kernel,
        grid=(27,),
        out_shape=[sds((27, 64, 1024), F32), sds((27, 64, 64), F32)],
        in_specs=[
            pl.BlockSpec((8, 1, 64, 128), lambda i: (0, slot_of(i), 0, 0)),
            pl.BlockSpec((640, 256), lambda i: (0, 0)),
        ],
        out_specs=[
            pl.BlockSpec((1, 64, 1024), lambda i: (i, 0, 0)),
            pl.BlockSpec((27, 64, 64), lambda i: (0, 0, 0)),
        ],
        compiler_params=pltpu.CompilerParams(vmem_limit_bytes=LIMIT),
        name="finish",
    )(gw, t)


def band_blocks(w):
    w9 = w.reshape(9, 192, 64)
    return jnp.concatenate([jnp.pad(w9, ((0, 0), (0, 64), (0, 0))), jnp.pad(w9, ((0, 0), (64, 0), (0, 0)))], axis=2)


def on_device(volume, conv1_weight, conv2_weight, cotangent):
    v = volume.reshape(32, 2048)
    cot = cotangent.reshape(64, 1024)
    shaped = conv1_weight.reshape(3, 3, 3, 64, 64)[::-1, ::-1, ::-1]
    back_one = jnp.swapaxes(shaped, 3, 4).reshape(27, 64, 64)
    dd = band_blocks(conv1_weight)
    ddb = band_blocks(back_one)
    vp, vn, call_, csl, woth = c1(v, cot, conv2_weight)
    pre, moved, lhs1 = k2(vp, v, vn, dd)
    mk = c3(moved)
    part, gm, piece = k4(mk, call_, csl, conv2_weight, woth)
    frecv, grecv, gw = c5(part, gm, piece)
    feat, gpn = k6(frecv, grecv, pre)
    gp, gn = c7(gpn)
    gvol, tsum = k8(gp, gpn, gn, lhs1, ddb)
    tall = c9(tsum)
    o2, o1 = k10(gw, tall)
    return feat.reshape(1, 1, 8, 8, 1024), gvol.reshape(1, 1, 32, 2048), o1, o2


def solution(mesh):
    return jax.shard_map(
        on_device,
        mesh=mesh,
        in_specs=(P("sample", "depth", None, None), P(), P(None, "depth", None), P("sample", "depth", None, None, None)),
        out_specs=(P("sample", "depth", None, None, None), P("sample", "depth", None, None), P(), P(None, "depth", None)),
        check_vma=False,
    )
```

```python
import functools
import math

import jax
import jax.numpy as jnp
from jax import lax
from jax.experimental import pallas as pl
from jax.experimental.pallas import tpu as pltpu
from jax.sharding import PartitionSpec as P

MESH = pl.DeviceIdType.MESH
F32 = jnp.float32
BF16 = jnp.bfloat16
ROOT = 0.7978845608028654
CUBIC = 0.044715
SCALE1 = 1.0 / math.sqrt(8 * 16 * 32 * 32)
SCALE2 = 1.0 / math.sqrt(8 * 16 * 8 * 8)
VM = pl.BlockSpec(memory_space=pltpu.VMEM)
ANY = pl.BlockSpec(memory_space=pl.ANY)
LIMIT = 60 * 1024 * 1024


def where_am_i():
    s = lax.axis_index("sample")
    d = lax.axis_index("depth")
    return s, d


def rcopy(src, dst, ss, rs, dev):
    return pltpu.make_async_remote_copy(
        src_ref=src, dst_ref=dst, send_sem=ss, recv_sem=rs, device_id=dev, device_id_type=MESH
    )


def depth_peer(d, jz, jy, jc):
    zh, y, c = d // 8, (d // 2) % 4, d % 2
    return ((zh + jz) % 2) * 8 + ((y + jy) % 4) * 2 + (c + jc) % 2


def depth_src(d, jz, jy, jc):
    zh, y, c = d // 8, (d // 2) % 4, d % 2
    return ((zh + jz) % 2) * 8 + ((y + 4 - jy) % 4) * 2 + (c + jc) % 2


def sample_peer(s, jz, jx):
    return ((s // 4 + jz) % 2) * 4 + (s % 4 + jx) % 4


def sample_src(s, jz, jx):
    return ((s // 4 + jz) % 2) * 4 + (s % 4 + 4 - jx) % 4


CHIPS = [(jz, jy) for jz in range(2) for jy in range(4) if (jz, jy) != (0, 0)]
SAMPS = [(jz, jx) for jz in range(2) for jx in range(4) if (jz, jx) != (0, 0)]


def barrier(devs):
    bar = pltpu.get_barrier_semaphore()
    for dev in devs:
        pl.semaphore_signal(bar, inc=1, device_id=dev, device_id_type=MESH)
    pl.semaphore_wait(bar, len(devs))


def onehot(shape, fn):
    row = lax.broadcasted_iota(jnp.int32, shape, 0)
    col = lax.broadcasted_iota(jnp.int32, shape, 1)
    return jnp.where(fn(row, col), 1.0, 0.0).astype(BF16)


def dot(a, b):
    return jnp.dot(a, b, preferred_element_type=F32)


def nat(rho):
    return 4 * (rho % 8) + rho // 8


def call(kern, outs, ins, scratch, name, cid=None, specs=None, out_specs=None, **kw):
    params = dict(vmem_limit_bytes=LIMIT)
    if cid is not None:
        params.update(collective_id=cid, has_side_effects=True)
    return pl.pallas_call(
        kern,
        out_shape=outs,
        in_specs=specs or [VM] * len(ins),
        out_specs=out_specs or [VM] * len(outs),
        scratch_shapes=scratch,
        compiler_params=pltpu.CompilerParams(**params),
        name=name,
    )(*ins)


def sds(shape, dtype=BF16):
    return jax.ShapeDtypeStruct(shape, dtype)


def depth_of(zh, y, c):
    return zh * 8 + y * 2 + c


def fill_rows(lhs, planes, perms):
    zero = jnp.zeros((32, 128), BF16)
    for a in range(3):
        for b in range(3):
            x = planes[a] if perms[b] is None else dot(perms[b], planes[a]).astype(BF16)
            xp = jnp.concatenate([zero, x, zero], axis=1)
            for j in range(8):
                lhs[pl.ds(j * 32, 32), pl.ds((3 * a + b) * 512, 512)] = xp[:, 256 * j : 256 * j + 512]


def edge_planes(prev, own, nxt, d):
    zero = jnp.zeros_like(own)
    return [jnp.where(d > 0, prev, zero), own, jnp.where(d < 15, nxt, zero)]


def gelu_parts(value):
    inner = ROOT * (value + CUBIC * value * value * value)
    return jnp.tanh(inner)


def row_shift(x, b):
    if b == 1:
        return x
    rows = x.shape[0]
    lane = lax.broadcasted_iota(jnp.int32, x.shape, 0) % 8
    if b == 0:
        return jnp.where(lane == 0, 0.0, pltpu.roll(x, 1, 0))
    return jnp.where(lane == 7, 0.0, pltpu.roll(x, rows - 1, 0))


def col_shift(x, c):
    if c == 1:
        return x
    zero = jnp.zeros((x.shape[0], 8, x.shape[2]), x.dtype)
    if c == 0:
        return jnp.concatenate([zero, x[:, :56]], axis=1)
    return jnp.concatenate([x[:, 8:], zero], axis=1)


def taps10(x, s2):
    n = x.shape[0]
    flat = x.astype(F32).reshape(n * 64, 128)
    for b in range(3):
        y = row_shift(flat, b).reshape(n, 64, 128)
        for c in range(3):
            s2[:, :, (3 * b + c) * 128 : (3 * b + c + 1) * 128] = col_shift(y, c).astype(BF16)


def put_band(band, ab, w3):
    zero = jnp.zeros((64, 64), BF16)
    left = jnp.concatenate([w3, zero], axis=0)
    right = jnp.concatenate([zero, w3], axis=0)
    both = jnp.concatenate([left, right], axis=1)
    band[pl.ds(ab * 512 + 64, 256), 0:128] = both
    band[pl.ds(ab * 512 + 192, 256), 128:256] = both


def fill_band(band, w1):
    band[...] = jnp.zeros_like(band)
    for ab in range(9):
        put_band(band, ab, w1[3 * ab : 3 * ab + 3].reshape(192, 64))


def fill_band_back(band, w1):
    band[...] = jnp.zeros_like(band)
    for ab in range(9):
        top = 3 * (8 - ab) + 2
        w3 = [jnp.transpose(w1[top - c].astype(F32)).astype(BF16) for c in range(3)]
        put_band(band, ab, jnp.concatenate(w3, axis=0))


CHUNKS = [(4 * q, min(4, 27 - 4 * q)) for q in range(7)]
XF = (0, 1, 2)
ZF = (3, 4, 5, 6)


def mega_kernel(
    v, cot, w1, w,
    feat, gvol, tout, gw,
    vp, vn, cotp, mine, cb, csl, wv, mk, moved, lhs, lhsb, band, bandb, s2o, s2, part, frecv,
    gm, grecv, acc, wacc, pre, ownf, psend, precv, gpn, gp, gn, tbuf, pbuf, pbuf2, own, rbuf, dbuf, rbuf2,
    wsem, hsem, asem, csem, xsem, msem, ssem, gsem, rsem, psem, nsend, nrecv, ksem, tsem,
):
    s, d = where_am_i()
    zh, y, c = d // 8, (d // 2) % 4, d % 2
    m = d // 2
    zl = s // 4
    up, down = (d + 1) % 16, (d + 15) % 16
    partner = depth_of(zh, y, 1 - c)
    wl = pltpu.make_async_copy(w, wv.at[:, c], wsem.at[0])
    wl.start()
    barrier(
        [(s, depth_peer(d, jz, jy, jc)) for jz in range(2) for jy in range(4) for jc in range(2) if (jz, jy, jc) != (0, 0, 0)]
        + [(sample_peer(s, jz, jx), d) for jz, jx in SAMPS]
    )
    late = []

    def spread(src_of, dst, sems, edge):
        k = d % 8
        for i, (jz, jy) in enumerate([(0, 0)] + CHIPS):
            t = depth_of((zh + jz) % 2, (y + jy) % 4, zh)
            cp = rcopy(src_of(t // 2), dst(k + edge), sems.at[i], sems.at[16 + k], (s, t))
            if i:
                cp.start()
                late.append((None, cp))
            else:

                @pl.when(t != d)
                def _(cp=cp):
                    cp.start()

                late.append((t != d, cp))
        if edge:
            rim = (d == 7) | (d == 8)
            for i, (jz, jy) in enumerate(CHIPS):
                t = depth_of((zh + jz) % 2, (y + jy) % 4, 1 - zh)
                cp = rcopy(src_of(t // 2), dst(zh * 9), sems.at[8 + i], sems.at[24], (s, t))

                @pl.when(rim)
                def _(cp=cp):
                    cp.start()

                late.append((rim, cp))

    def spread_local(value, dst_ref, edge):
        @pl.when(c == zh)
        def _():
            dst_ref(d % 8 + edge, value)

        if edge:

            @pl.when((d == 7) | (d == 8))
            def _():
                dst_ref(zh * 9, value)

    def spread_wait(dst, sems, edge):
        for k in range(8):

            @pl.when(8 * c + k != d)
            def _(k=k):
                rcopy(dst(k + edge), dst(k + edge), sems.at[0], sems.at[16 + k], (s, partner)).wait_recv()

        if edge:
            q = 9 - 9 * c

            @pl.when(8 - c != d)
            def _():
                rcopy(dst(q), dst(q), sems.at[0], sems.at[24], (s, partner)).wait_recv()

    def to_owner(src, dst, sems, lo=0):
        for i in range(8):
            p = 8 * c + i
            cp = rcopy(src.at[i], dst.at[m], sems.at[i], sems.at[8 + m], (s, p))

            @pl.when(p != d)
            def _(cp=cp):
                cp.start()

            @pl.when(p == d)
            def _(i=i):
                dst[m] = src[i]

            late.append((p != d, cp))

    def owner_wait(dst, sems):
        for j in range(8):

            @pl.when(2 * j + zh != d)
            def _(j=j):
                rcopy(dst.at[j], dst.at[j], sems.at[0], sems.at[8 + j], (s, partner)).wait_recv()

    halo = [rcopy(v, vp, hsem.at[0], hsem.at[1], (s, up)), rcopy(v, vn, hsem.at[2], hsem.at[3], (s, down))]
    for h in halo:
        h.start()
    wx = rcopy(w, wv.at[:, c], wsem.at[1], wsem.at[2], (s, partner))
    wx.start()
    perm64 = onehot((64, 64), lambda u, q: q == (u % 8) * 8 + u // 8)
    cotp[...] = dot(perm64, cot[...]).astype(BF16)
    for i, (jz, jx) in enumerate(SAMPS):
        t = sample_peer(s, jz, jx)
        cp = rcopy(cotp.at[:, pl.ds(pl.multiple_of(t * 128, 128), 128)], mine.at[s], asem.at[i], asem.at[7 + i], (t, d))
        cp.start()
        late.append((None, cp))
    spread(lambda t: cotp, lambda k: cb.at[k], csem, 1)

    def put_cb(k, value):
        cb[k] = value

    spread_local(cotp[...], put_cb, 1)
    mine[s] = cotp[:, pl.ds(pl.multiple_of(s * 128, 128), 128)]
    cb[9 * c] = jnp.zeros((64, 1024), BF16)
    mk[:, 9 * c] = jnp.zeros((8, 64, 128), BF16)

    fill_band(band, w1)
    perms = [onehot((32, 32), lambda rho, i, b=b: i == nat(rho) + b - 1) for b in range(3)]
    for h in halo:
        h.wait()
    fill_rows(lhs, edge_planes(vp[...], v[...], vn[...], d), perms)
    res = dot(lhs[...], band[...])
    for r in range(4):
        z = jnp.concatenate([res[j * 32 + r * 8 : j * 32 + r * 8 + 8] for j in range(8)], axis=0)
        pre[r] = z
        hid = (0.5 * z * (1.0 + gelu_parts(z))).astype(BF16)
        moved[2 * r] = hid[:, 0:128]
        moved[2 * r + 1] = hid[:, 128:256]
    spread(lambda t: moved.at[t], lambda k: mk.at[s, k], msem, 1)

    def put_mk(k, value):
        mk[s, k] = value

    spread_local(moved[m], put_mk, 1)

    for i, (jz, jx) in enumerate(SAMPS):
        t = sample_src(s, jz, jx)
        rcopy(mine.at[t], mine.at[t], asem.at[i], asem.at[7 + i], (t, d)).wait_recv()
    spread(lambda t: mine, lambda k: csl.at[k], xsem, 0)

    def put_csl(k, value):
        csl[k] = value

    spread_local(mine[...], put_csl, 0)
    fill_band_back(bandb, w1)
    wacc[...] = jnp.zeros_like(wacc)

    spread_wait(lambda k: mk.at[s, k], msem, 1)
    nine = pl.ds(1 - c, 9)
    for i in range(1, 8):
        cp = rcopy(mk.at[s, nine], mk.at[s, nine], ssem.at[i - 1], ssem.at[6 + i], (sample_peer(s, i // 4, i % 4), d))
        cp.start()
        late.append((None, cp))
    taps10(mk[s], s2o)

    wl.wait()
    wx.wait()
    spread_wait(lambda k: cb.at[k], csem, 1)

    def back(i, _):
        tot = jnp.zeros((512, 384), F32)
        for a in range(3):
            rows = cb[2 - a : 10 - a].reshape(512, 1024)
            wt = wv[pl.ds(9 * a + 3 * i, 3)].reshape(384, 1024)
            tot = tot + lax.dot_general(rows, wt, (((1,), (1,)), ((), ())), preferred_element_type=F32)
        for j in range(3):
            acc[3 * i + j] = tot[:, 128 * j : 128 * j + 128]
        return 0

    lax.fori_loop(0, 3, back, 0)
    total = jnp.zeros((8, 64, 128), F32)
    for b in range(3):
        inner = jnp.zeros((8, 64, 128), F32)
        for cc in range(3):
            inner = inner + col_shift(acc[3 * b + cc].reshape(8, 64, 128), 2 - cc)
        total = total + row_shift(inner.reshape(512, 128), 2 - b).reshape(8, 64, 128)
    gm[...] = total.astype(BF16)
    to_owner(gm, grecv, gsem)

    spread_wait(lambda k: csl.at[k], xsem, 0)

    def wpart(t, ref):
        ct = jnp.transpose(csl[:, t].reshape(512, 128).astype(F32)).astype(BF16)
        for a in range(3):
            wacc[:, 1152 * a : 1152 * a + 1152] += dot(ct, ref[a : a + 8].reshape(512, 1152))

    wpart(s, s2o)

    def wgrad(i, _):
        t = ((zl + i // 4) % 2) * 4 + (s % 4 + 4 - i % 4) % 4
        rcopy(mk.at[t, nine], mk.at[t, nine], ssem.at[i - 1], ssem.at[6 + i], (s, partner)).wait_recv()
        taps10(mk[t], s2)
        wpart(t, s2)
        return 0

    lax.fori_loop(1, 8, wgrad, 0)

    pcp = []
    for q, (lo, n) in enumerate(CHUNKS):
        for t in range(lo, lo + n):
            x = jnp.transpose(wacc[:, t * 128 : t * 128 + 128] * SCALE2)
            ownf[t] = jnp.where(c == 0, x[0:64], x[64:128])
            psend[t] = jnp.where(c == 0, x[64:128], x[0:64]).astype(BF16)
        cp = rcopy(psend.at[pl.ds(lo, n)], precv.at[pl.ds(lo, n)], psem.at[q], psem.at[7 + q], (s, partner))
        cp.start()
        pcp.append(cp)

    xp, xm, zo = sample_peer(s, 0, 1), sample_peer(s, 0, 3), sample_peer(s, 1, 0)
    x2 = sample_peer(s, 0, 2)
    oxp, oxm, ox2 = sample_peer(s, 1, 1), sample_peer(s, 1, 3), sample_peer(s, 1, 2)

    def nsem(q, kind):
        return nsend.at[7 * q + kind], nrecv.at[7 * q + kind]

    def send(q, kind, block, dev):
        ref = gw.at[block, pl.ds(*CHUNKS[q])]
        cp = rcopy(ref, ref, *nsem(q, kind), (dev, d))
        cp.start()
        late.append((None, cp))

    def recv(q, kind, block):
        ref = gw.at[block, pl.ds(*CHUNKS[q])]
        rcopy(ref, ref, *nsem(q, kind), (s, partner)).wait_recv()

    for q, (lo, n) in enumerate(CHUNKS):
        pcp[q].wait()
        gw[s, pl.ds(lo, n)] = (ownf[pl.ds(lo, n)] + precv[pl.ds(lo, n)].astype(F32)).astype(BF16)
        if q in ZF:
            send(q, 0, s, zo)
        send(q, 1, s, xp)
        send(q, 2, s, xm)
    for q in XF:
        send(q, 0, s, zo)

    owner_wait(grecv, gsem)
    gpf = []
    for r in range(4):
        z = pre[r]
        th = gelu_parts(z)
        slope = 0.5 * (1.0 + th) + 0.5 * z * (1.0 - th * th) * ROOT * (1.0 + 3.0 * CUBIC * z * z)
        gpf.append(jnp.concatenate([grecv[2 * r], grecv[2 * r + 1]], axis=1).astype(F32) * slope)
    for j in range(8):
        rows = jnp.concatenate([gpf[r][8 * j : 8 * j + 8] for r in range(4)], axis=0)
        gpn[:, 256 * j : 256 * j + 256] = rows.astype(BF16)
    ghalo = [rcopy(gpn, gp, hsem.at[4], hsem.at[5], (s, up)), rcopy(gpn, gn, hsem.at[6], hsem.at[7], (s, down))]
    for h in ghalo:
        h.start()

    gx = jnp.concatenate([gpn[:, 256 * j : 256 * j + 256] for j in range(8)], axis=0)
    gt = jnp.transpose(gx.astype(F32)).astype(BF16)
    for ab in range(9):
        o = dot(gt, lhs[:, 512 * ab : 512 * ab + 512])
        even = o[0:64, 0:256] + o[128:192, 128:384]
        t = o[64:128, 128:384] + o[192:256, 256:512] + pltpu.roll(even, 192, 1)
        tbuf[64 * ab : 64 * ab + 64] = (t * SCALE1).astype(BF16)
    tbuf[576:640] = jnp.zeros((64, 256), BF16)
    lane = pl.ds(pl.multiple_of(c * 128, 128), 128)
    lane2 = pl.ds(pl.multiple_of(128 - c * 128, 128), 128)
    k1 = rcopy(tbuf.at[:, lane2], pbuf, ksem.at[0], ksem.at[1], (s, partner))
    k1.start()

    for q in XF:
        recv(q, 1, xm)
        if q % 2 == 0:
            send(q, 3, xm, xp)
        send(q, 4, xm, zo)
        recv(q, 2, xp)
        if q % 2:
            send(q, 3, xp, xm)
        send(q, 5, xp, zo)

    k1.wait()
    own[...] = (tbuf[:, lane].astype(F32) + pbuf[...].astype(F32)).astype(BF16)
    k2s = []
    for i, (jz, jy) in enumerate(CHIPS):
        t = depth_peer(d, jz, jy, 0)
        k2s.append(rcopy(own.at[pl.ds(pl.multiple_of((t // 2) * 80, 16), 80)], rbuf.at[i], tsem.at[i], tsem.at[7 + i], (s, t)))
        k2s[-1].start()

    for q in ZF:
        recv(q, 0, zo)
        send(q, 4, zo, xp)
        send(q, 5, zo, xm)

    def fwd(i, _):
        tot = jnp.zeros((256, 1024), F32)
        for a in range(3):
            tot = tot + dot(s2o[pl.ds(4 * i + a, 4)].reshape(256, 1152), wv[9 * a : 9 * a + 9].reshape(1152, 1024))
        part[pl.ds(4 * i, 4)] = tot.astype(BF16).reshape(4, 64, 1024)
        return 0

    lax.fori_loop(0, 2, fwd, 0)
    to_owner(part, frecv, rsem)

    for q in ZF:
        recv(q, 1, xm)
        if q % 2 == 0:
            send(q, 3, xm, xp)
        recv(q, 2, xp)
        if q % 2:
            send(q, 3, xp, xm)
    for q in XF:
        recv(q, 3, x2)
        send(q, 6, x2, zo)

    piece = pl.ds(pl.multiple_of(m * 80, 16), 80)
    tot = own[piece].astype(F32)
    for i in range(7):
        k2s[i].wait()
        tot = tot + rbuf[i].astype(F32)
    dbuf[7] = tot.astype(BF16)
    k3s = []
    for i, (jz, jx) in enumerate(SAMPS):
        k3s.append(rcopy(dbuf.at[7], dbuf.at[i], tsem.at[14 + i], tsem.at[21 + i], (sample_peer(s, jz, jx), d)))
        k3s[-1].start()

    for h in ghalo:
        h.wait()
    perms = [onehot((32, 32), lambda u, q, b=b: nat(q) == nat(u) + b - 1) for b in range(3)]
    perms[1] = None
    fill_rows(lhsb, edge_planes(gp[...], gpn[...], gn[...], d), perms)
    res = dot(lhsb[...], bandb[...]).astype(BF16)
    wide = jnp.concatenate([res[32 * j : 32 * j + 32] for j in range(8)], axis=1)
    gvol[...] = dot(onehot((32, 32), lambda i, q: nat(q) == i), wide).astype(BF16)

    for q in ZF:
        recv(q, 4, oxm)
        if q % 2 == 0:
            send(q, 6, oxm, xp)
        recv(q, 5, oxp)
        if q % 2:
            send(q, 6, oxp, xm)

    for x in k3s:
        x.wait()
    tot = None
    for j in range(8):
        idx = ((j // 4 + zl) % 2) * 4 + (s % 4 + 4 - j % 4) % 4
        idx = jnp.where(idx == 0, 7, idx - 1)
        val = dbuf[idx].astype(F32)
        tot = val if tot is None else tot + val
    own[piece] = tot.astype(BF16)
    k4s = []
    for i, (jz, jy) in enumerate(CHIPS):
        k4s.append(rcopy(own.at[piece], rbuf2.at[i], tsem.at[28 + i], tsem.at[35 + i], (s, depth_peer(d, jz, jy, 0))))
        k4s[-1].start()

    owner_wait(frecv, rsem)
    tot = frecv[0].astype(F32)
    for i in range(1, 8):
        tot = tot + frecv[i].astype(F32)
    feat[...] = dot(perm64, tot.astype(BF16)).astype(BF16)

    for i, (jz, jy) in enumerate(CHIPS):
        k4s[i].wait()
        own[pl.ds(pl.multiple_of((depth_src(d, jz, jy, 0) // 2) * 80, 16), 80)] = rbuf2[i]
    k5 = rcopy(own, pbuf2, ksem.at[2], ksem.at[3], (s, partner))
    k5.start()
    tout[:, lane] = own[...]
    k5.wait()
    tout[:, lane2] = pbuf2[...]

    for q in XF:
        recv(q, 0, zo)
        recv(q, 4, oxm)
        recv(q, 5, oxp)
        recv(q, 6, ox2)
    for q in ZF:
        recv(q, 3, x2)
        recv(q, 6, ox2)
    for cond, cp in late:
        if cond is None:
            cp.wait_send()
        else:

            @pl.when(cond)
            def _(cp=cp):
                cp.wait_send()


def mega(v, cot, w1, w):
    dma = pltpu.SemaphoreType.DMA
    vm = lambda *shape: pltpu.VMEM(shape, BF16)
    vf = lambda *shape: pltpu.VMEM(shape, F32)
    scratch = [
        vm(32, 2048), vm(32, 2048), vm(64, 1024), vm(8, 64, 128), vm(10, 64, 1024), vm(8, 8, 64, 128),
        vm(27, 2, 64, 1024), vm(8, 10, 64, 128), vm(8, 64, 128), vm(256, 4608), vm(256, 4608), vm(4608, 256),
        vm(4608, 256), vm(10, 64, 1152), vm(10, 64, 1152), vm(8, 64, 1024), vm(8, 64, 1024),
        vm(8, 64, 128), vm(8, 64, 128), vf(9, 512, 128), vf(128, 3456), vf(4, 64, 256), vf(27, 64, 128),
        vm(27, 64, 128), vm(27, 64, 128), vm(32, 2048), vm(32, 2048), vm(32, 2048), vm(640, 256), vm(640, 128),
        vm(640, 128), vm(640, 128), vm(7, 80, 128), vm(8, 80, 128), vm(7, 80, 128),
        dma((3,)), dma((8,)), dma((14,)), dma((25,)), dma((25,)), dma((25,)), dma((14,)), dma((16,)), dma((16,)),
        dma((14,)), dma((49,)), dma((49,)), dma((4,)), dma((42,)),
    ]
    return pl.pallas_call(
        mega_kernel,
        out_shape=[sds((64, 1024)), sds((32, 2048)), sds((640, 256)), sds((8, 27, 64, 128))],
        in_specs=[VM, VM, VM, ANY],
        out_specs=[VM] * 4,
        scratch_shapes=scratch,
        compiler_params=pltpu.CompilerParams(vmem_limit_bytes=LIMIT, collective_id=1, has_side_effects=True),
        name="step",
    )(v, cot, w1, w)


def finish_kernel(gw, t, f, g, o2, o1, of, og):
    for q in range(8):
        o2[:, :, 128 * q : 128 * q + 128] = gw[q].astype(F32)

    @pl.when(pl.program_id(0) == 0)
    def _():
        of[...] = f[...]
        og[...] = g[...]
        for ab in range(9):
            x = jnp.transpose(t[64 * ab : 64 * ab + 64].astype(F32))
            o1[3 * ab : 3 * ab + 3] = x[0:192].reshape(3, 64, 64)


def finish(gw, t, f, g):
    whole = lambda *shape: pl.BlockSpec(shape, lambda i: (0,) * len(shape))
    return pl.pallas_call(
        finish_kernel,
        grid=(9,),
        out_shape=[sds((27, 64, 1024), F32), sds((27, 64, 64), F32), sds((64, 1024)), sds((32, 2048))],
        in_specs=[pl.BlockSpec((8, 3, 64, 128), lambda i: (0, i, 0, 0)), whole(640, 256), whole(64, 1024), whole(32, 2048)],
        out_specs=[pl.BlockSpec((3, 64, 1024), lambda i: (i, 0, 0)), whole(27, 64, 64), whole(64, 1024), whole(32, 2048)],
        compiler_params=pltpu.CompilerParams(vmem_limit_bytes=LIMIT),
        name="finish",
    )(gw, t, f, g)


def on_device(volume, conv1_weight, conv2_weight, cotangent):
    feat, gvol, tall, gw = mega(volume.reshape(32, 2048), cotangent.reshape(64, 1024), conv1_weight, conv2_weight)
    o2, o1, feat, gvol = finish(gw, tall, feat, gvol)
    return feat.reshape(1, 1, 8, 8, 1024), gvol.reshape(1, 1, 32, 2048), o1, o2


def solution(mesh):
    return jax.shard_map(
        on_device,
        mesh=mesh,
        in_specs=(P("sample", "depth", None, None), P(), P(None, "depth", None), P("sample", "depth", None, None, None)),
        out_specs=(P("sample", "depth", None, None, None), P("sample", "depth", None, None), P(), P(None, "depth", None)),
        check_vma=False,
    )
```

```python
import functools
import math

import jax
import jax.numpy as jnp
from jax import lax
from jax.experimental import pallas as pl
from jax.experimental.pallas import tpu as pltpu
from jax.sharding import PartitionSpec as P

MESH = pl.DeviceIdType.MESH
F32 = jnp.float32
BF16 = jnp.bfloat16
ROOT = 0.7978845608028654
CUBIC = 0.044715
SCALE1 = 1.0 / math.sqrt(8 * 16 * 32 * 32)
SCALE2 = 1.0 / math.sqrt(8 * 16 * 8 * 8)
VM = pl.BlockSpec(memory_space=pltpu.VMEM)
ANY = pl.BlockSpec(memory_space=pl.ANY)
LIMIT = 60 * 1024 * 1024


def where_am_i():
    s = lax.axis_index("sample")
    d = lax.axis_index("depth")
    return s, d


def rcopy(src, dst, ss, rs, dev):
    return pltpu.make_async_remote_copy(
        src_ref=src, dst_ref=dst, send_sem=ss, recv_sem=rs, device_id=dev, device_id_type=MESH
    )


def depth_peer(d, jz, jy, jc):
    zh, y, c = d // 8, (d // 2) % 4, d % 2
    return ((zh + jz) % 2) * 8 + ((y + jy) % 4) * 2 + (c + jc) % 2


def depth_src(d, jz, jy, jc):
    zh, y, c = d // 8, (d // 2) % 4, d % 2
    return ((zh + jz) % 2) * 8 + ((y + 4 - jy) % 4) * 2 + (c + jc) % 2


def sample_peer(s, jz, jx):
    return ((s // 4 + jz) % 2) * 4 + (s % 4 + jx) % 4


def sample_src(s, jz, jx):
    return ((s // 4 + jz) % 2) * 4 + (s % 4 + 4 - jx) % 4


CHIPS = [(jz, jy) for jz in range(2) for jy in range(4) if (jz, jy) != (0, 0)]
SAMPS = [(jz, jx) for jz in range(2) for jx in range(4) if (jz, jx) != (0, 0)]


def barrier(devs):
    bar = pltpu.get_barrier_semaphore()
    for dev in devs:
        pl.semaphore_signal(bar, inc=1, device_id=dev, device_id_type=MESH)
    pl.semaphore_wait(bar, len(devs))


def onehot(shape, fn):
    row = lax.broadcasted_iota(jnp.int32, shape, 0)
    col = lax.broadcasted_iota(jnp.int32, shape, 1)
    return jnp.where(fn(row, col), 1.0, 0.0).astype(BF16)


def dot(a, b):
    return jnp.dot(a, b, preferred_element_type=F32)


def nat(rho):
    return 4 * (rho % 8) + rho // 8


def call(kern, outs, ins, scratch, name, cid=None, specs=None, out_specs=None, **kw):
    params = dict(vmem_limit_bytes=LIMIT)
    if cid is not None:
        params.update(collective_id=cid, has_side_effects=True)
    return pl.pallas_call(
        kern,
        out_shape=outs,
        in_specs=specs or [VM] * len(ins),
        out_specs=out_specs or [VM] * len(outs),
        scratch_shapes=scratch,
        compiler_params=pltpu.CompilerParams(**params),
        name=name,
    )(*ins)


def sds(shape, dtype=BF16):
    return jax.ShapeDtypeStruct(shape, dtype)


def depth_of(zh, y, c):
    return zh * 8 + y * 2 + c


def fill_rows(lhs, planes, perms):
    zero = jnp.zeros((32, 128), BF16)
    for a in range(3):
        for b in range(3):
            x = planes[a] if perms[b] is None else dot(perms[b], planes[a]).astype(BF16)
            xp = jnp.concatenate([zero, x, zero], axis=1)
            for j in range(8):
                lhs[pl.ds(j * 32, 32), pl.ds((3 * a + b) * 512, 512)] = xp[:, 256 * j : 256 * j + 512]


def edge_planes(prev, own, nxt, d):
    zero = jnp.zeros_like(own)
    return [jnp.where(d > 0, prev, zero), own, jnp.where(d < 15, nxt, zero)]


def gelu_parts(value):
    inner = ROOT * (value + CUBIC * value * value * value)
    return jnp.tanh(inner)


def row_shift(x, b):
    if b == 1:
        return x
    rows = x.shape[0]
    lane = lax.broadcasted_iota(jnp.int32, x.shape, 0) % 8
    if b == 0:
        return jnp.where(lane == 0, 0.0, pltpu.roll(x, 1, 0))
    return jnp.where(lane == 7, 0.0, pltpu.roll(x, rows - 1, 0))


def col_shift(x, c):
    if c == 1:
        return x
    zero = jnp.zeros((x.shape[0], 8, x.shape[2]), x.dtype)
    if c == 0:
        return jnp.concatenate([zero, x[:, :56]], axis=1)
    return jnp.concatenate([x[:, 8:], zero], axis=1)


def taps10(x, s2):
    n = x.shape[0]
    flat = x.astype(F32).reshape(n * 64, 128)
    for b in range(3):
        y = row_shift(flat, b).reshape(n, 64, 128)
        for c in range(3):
            s2[:, :, (3 * b + c) * 128 : (3 * b + c + 1) * 128] = col_shift(y, c).astype(BF16)


def put_band(band, ab, w3):
    zero = jnp.zeros((64, 64), BF16)
    left = jnp.concatenate([w3, zero], axis=0)
    right = jnp.concatenate([zero, w3], axis=0)
    both = jnp.concatenate([left, right], axis=1)
    band[pl.ds(ab * 512 + 64, 256), 0:128] = both
    band[pl.ds(ab * 512 + 192, 256), 128:256] = both


def fill_band(band, w1):
    band[...] = jnp.zeros_like(band)
    for ab in range(9):
        put_band(band, ab, w1[3 * ab : 3 * ab + 3].reshape(192, 64))


def fill_band_back(band, w1):
    band[...] = jnp.zeros_like(band)
    for ab in range(9):
        top = 3 * (8 - ab) + 2
        w3 = [jnp.transpose(w1[top - c].astype(F32)).astype(BF16) for c in range(3)]
        put_band(band, ab, jnp.concatenate(w3, axis=0))


STOP = None


class Done(Exception):
    pass


CHUNKS = [(4 * q, min(4, 27 - 4 * q)) for q in range(7)]
XF = (0, 1, 2)
ZF = (3, 4, 5, 6)


def mega_kernel(*refs):
    try:
        mega_body(*refs)
    except Done:
        pass


def mega_body(
    v, cot, w1, w,
    feat, gvol, o1, gw,
    vp, vn, cotp, mine, cb, csl, wv, mk, moved, lhs, lhsb, band, bandb, s2o, s2, part, frecv,
    gm, grecv, acc, wacc, pre, ownf, psend, precv, gpn, gp, gn, tbuf, pbuf, pbuf2, own, rbuf, dbuf, rbuf2,
    wsem, hsem, asem, csem, xsem, msem, ssend, srecv, gsem, rsem, psem, nsend, nrecv, ksem, tsem,
):
    s, d = where_am_i()
    zh, y, c = d // 8, (d // 2) % 4, d % 2
    m = d // 2
    zl = s // 4
    up, down = (d + 1) % 16, (d + 15) % 16
    partner = depth_of(zh, y, 1 - c)
    yp, ym = depth_of(zh, (y + 1) % 4, c), depth_of(zh, (y + 3) % 4, c)
    late = []
    pend = {}

    def stop(k):
        if STOP == k:
            for fn in list(pend.values()):
                fn()
            for cond, cp in late:
                wait_late(cond, cp)
            raise Done

    def wait(k):
        pend.pop(k)()

    def wait_late(cond, cp):
        if cond is None:
            cp.wait_send()
        else:

            @pl.when(cond)
            def _():
                cp.wait_send()

    def go(src, dst, ss, rs, dev):
        cp = rcopy(src, dst, ss, rs, dev)
        cp.start()
        late.append((None, cp))

    def got(ref, ss, rs):
        rcopy(ref, ref, ss, rs, (s, partner)).wait_recv()

    def spread(src_of, dst, sems):
        k = d % 8
        for i, (jz, jy) in enumerate([(0, 0)] + CHIPS):
            t = depth_of((zh + jz) % 2, (y + jy) % 4, zh)
            if i:
                go(src_of(t // 2), dst(k + 1), sems.at[i], sems.at[16 + k], (s, t))
            else:
                cp = rcopy(src_of(t // 2), dst(k + 1), sems.at[i], sems.at[16 + k], (s, t))

                @pl.when(t != d)
                def _(cp=cp):
                    cp.start()

                late.append((t != d, cp))
        rim = (d == 7) | (d == 8)
        for i, (jz, jy) in enumerate(CHIPS):
            t = depth_of((zh + jz) % 2, (y + jy) % 4, 1 - zh)
            cp = rcopy(src_of(t // 2), dst(zh * 9), sems.at[8 + i], sems.at[24], (s, t))

            @pl.when(rim)
            def _(cp=cp):
                cp.start()

            late.append((rim, cp))

    def spread_wait(dst, sems):
        for k in range(8):

            @pl.when(8 * c + k != d)
            def _(k=k):
                got(dst(k + 1), sems.at[0], sems.at[16 + k])

        q = 9 - 9 * c

        @pl.when(8 - c != d)
        def _():
            got(dst(q), sems.at[0], sems.at[24])

    def home_send(src, buf, sems, edge):
        k = d % 8 + edge
        here, there = depth_of(zh, y, zh), depth_of(1 - zh, y, zh)
        go(src, buf.at[k], sems.at[1], sems.at[4 + c], (s, there))
        cp = rcopy(src, buf.at[k], sems.at[0], sems.at[4 + c], (s, here))

        @pl.when(c != zh)
        def _():
            cp.start()

        late.append((c != zh, cp))

        @pl.when(c == zh)
        def _():
            buf[k] = src[...]

    def home_wait(buf, sems, edge):
        for j in range(2):

            @pl.when((zh != c) | (c != j))
            def _(j=j):
                got(buf.at[2 * y + j + edge], sems.at[0], sems.at[4 + j])

    def ring_send(buf, sems, edge):
        two = buf.at[pl.ds(2 * y + edge, 2)]
        go(two, two, sems.at[2], sems.at[6], (s, yp))
        go(two, two, sems.at[3], sems.at[7], (s, ym))

    def ring_relay(buf, sems, edge):
        lo, hi = (y + 3) % 4, (y + 1) % 4
        got(buf.at[pl.ds(2 * lo + edge, 2)], sems.at[2], sems.at[6])
        one = buf.at[2 * lo + edge]
        go(one, one, sems.at[8], sems.at[10], (s, yp))
        got(buf.at[pl.ds(2 * hi + edge, 2)], sems.at[3], sems.at[7])
        one = buf.at[2 * hi + 1 + edge]
        go(one, one, sems.at[9], sems.at[11], (s, ym))

    def ring_wait(buf, sems, edge):
        far = (y + 2) % 4
        got(buf.at[2 * far + edge], sems.at[8], sems.at[10])
        got(buf.at[2 * far + 1 + edge], sems.at[9], sems.at[11])

    def to_owner(src, dst, sems):
        for i in range(8):
            p = 8 * c + i
            cp = rcopy(src.at[i], dst.at[m], sems.at[i], sems.at[8 + m], (s, p))

            @pl.when(p != d)
            def _(cp=cp):
                cp.start()

            @pl.when(p == d)
            def _(i=i):
                dst[m] = src[i]

            late.append((p != d, cp))

    def owner_wait(dst, sems):
        for j in range(8):

            @pl.when(2 * j + zh != d)
            def _(j=j):
                got(dst.at[j], sems.at[0], sems.at[8 + j])

    xp, xm, x2 = sample_peer(s, 0, 1), sample_peer(s, 0, 3), sample_peer(s, 0, 2)
    zo, oxp, oxm, ox2 = sample_peer(s, 1, 0), sample_peer(s, 1, 1), sample_peer(s, 1, 3), sample_peer(s, 1, 2)

    class Gather:
        def __init__(self, ref, xf, zf, ss, rs):
            self.ref, self.xf, self.zf, self.ss, self.rs = ref, xf, zf, ss, rs

        def send(self, q, kind, block, dev):
            r = self.ref(block, q)
            go(r, r, self.ss.at[7 * q + kind], self.rs.at[7 * q + kind], (dev, d))

        def recv(self, q, kind, block):
            got(self.ref(block, q), self.ss.at[7 * q + kind], self.rs.at[7 * q + kind])

        def start(self, q):
            if q in self.zf:
                self.send(q, 0, s, zo)
            self.send(q, 1, s, xp)
            self.send(q, 2, s, xm)

        def start_z(self):
            for q in self.xf:
                self.send(q, 0, s, zo)

        def near(self, q):
            self.recv(q, 1, xm)
            if q % 2 == 0:
                self.send(q, 3, xm, xp)
            if q in self.xf:
                self.send(q, 4, xm, zo)
            self.recv(q, 2, xp)
            if q % 2:
                self.send(q, 3, xp, xm)
            if q in self.xf:
                self.send(q, 5, xp, zo)

        def across(self, q):
            self.recv(q, 0, zo)
            self.send(q, 4, zo, xp)
            self.send(q, 5, zo, xm)

        def far(self, q):
            self.recv(q, 3, x2)
            self.send(q, 6, x2, zo)

        def turn(self, q):
            self.recv(q, 4, oxm)
            if q % 2 == 0:
                self.send(q, 6, oxm, xp)
            self.recv(q, 5, oxp)
            if q % 2:
                self.send(q, 6, oxp, xm)

        def finish(self):
            for q in self.xf:
                self.recv(q, 0, zo)
                self.recv(q, 4, oxm)
                self.recv(q, 5, oxp)
                self.recv(q, 6, ox2)
            for q in self.zf:
                self.recv(q, 3, x2)
                self.recv(q, 6, ox2)

        def rest(self):
            for q in self.xf:
                self.near(q)
            for q in self.zf:
                self.across(q)
            for q in self.zf:
                self.near(q)
            for q in self.xf:
                self.far(q)
            for q in self.zf:
                self.turn(q)
            self.finish()

    agm = Gather(lambda b, q: mk.at[b, pl.ds(1 - c + 3 * q, 3)], (0,), (1, 2), ssend, srecv)
    agw = Gather(
        lambda b, q: gw.at[pl.ds(*CHUNKS[q]), :, pl.ds(pl.multiple_of(b * 128, 128), 128)], XF, ZF, nsend, nrecv
    )

    wl = pltpu.make_async_copy(w, wv.at[:, c], wsem.at[0])
    wl.start()
    pend["wl"] = wl.wait
    bar = pltpu.get_barrier_semaphore()
    friends = [
        (s, depth_peer(d, jz, jy, jc)) for jz in range(2) for jy in range(4) for jc in range(2) if (jz, jy, jc) != (0, 0, 0)
    ] + [(sample_peer(s, jz, jx), d) for jz, jx in SAMPS]
    for dev in friends:
        pl.semaphore_signal(bar, inc=1, device_id=dev, device_id_type=MESH)
    perm64 = onehot((64, 64), lambda u, q: q == (u % 8) * 8 + u // 8)
    cotp[...] = dot(perm64, cot[...]).astype(BF16)
    mine[s] = cotp[:, pl.ds(pl.multiple_of(s * 128, 128), 128)]
    cb[9 * c] = jnp.zeros((64, 1024), BF16)
    mk[:, 9 * c] = jnp.zeros((8, 64, 128), BF16)
    fill_band(band, w1)
    pl.semaphore_wait(bar, len(friends))
    stop(0)

    halo = [rcopy(v, vp, hsem.at[0], hsem.at[1], (s, up)), rcopy(v, vn, hsem.at[2], hsem.at[3], (s, down))]
    for h in halo:
        h.start()
    pend["halo"] = lambda: [h.wait() for h in halo]
    home_send(cotp, cb, csem, 1)
    for i, (jz, jx) in enumerate(SAMPS):
        t = sample_peer(s, jz, jx)
        go(cotp.at[:, pl.ds(pl.multiple_of(t * 128, 128), 128)], mine.at[s], asem.at[i], asem.at[7 + i], (t, d))
    wx = rcopy(w, wv.at[:, c], wsem.at[1], wsem.at[2], (s, partner))
    wx.start()
    pend["wx"] = wx.wait

    def mine_wait():
        for i, (jz, jx) in enumerate(SAMPS):
            got(mine.at[sample_src(s, jz, jx)], asem.at[i], asem.at[7 + i])

    pend["mine"] = mine_wait

    perms = [onehot((32, 32), lambda rho, i, b=b: i == nat(rho) + b - 1) for b in range(3)]
    wait("halo")
    home_wait(cb, csem, 1)
    ring_send(cb, csem, 1)
    fill_rows(lhs, edge_planes(vp[...], v[...], vn[...], d), perms)
    res = dot(lhs[...], band[...])
    for r in range(4):
        z = jnp.concatenate([res[j * 32 + r * 8 : j * 32 + r * 8 + 8] for j in range(8)], axis=0)
        pre[r] = z
        hid = (0.5 * z * (1.0 + gelu_parts(z))).astype(BF16)
        moved[2 * r] = hid[:, 0:128]
        moved[2 * r + 1] = hid[:, 128:256]
    spread(lambda t: moved.at[t], lambda k: mk.at[s, k], msem)
    pend["mk"] = lambda: spread_wait(lambda k: mk.at[s, k], msem)

    @pl.when(c == zh)
    def _():
        mk[s, d % 8 + 1] = moved[m]

    @pl.when((d == 7) | (d == 8))
    def _():
        mk[s, zh * 9] = moved[m]

    wait("mine")
    home_send(mine, csl, xsem, 0)
    if STOP == 1:
        pend["a"] = lambda: (ring_relay(cb, csem, 1), home_wait(csl, xsem, 0), ring_wait(cb, csem, 1))
    stop(1)
    fill_band_back(bandb, w1)
    ring_relay(cb, csem, 1)

    wait("mk")
    for q in range(3):
        agm.start(q)
    agm.start_z()
    home_wait(csl, xsem, 0)
    ring_send(csl, xsem, 0)
    if STOP == 2:
        pend["a"] = lambda: (ring_relay(csl, xsem, 0), ring_wait(cb, csem, 1), ring_wait(csl, xsem, 0), agm.rest())
    stop(2)
    taps10(mk[s], s2o)
    wacc[...] = jnp.zeros_like(wacc)
    ring_wait(cb, csem, 1)
    rim_out = cb.at[8 - 7 * c]
    go(rim_out, cb.at[9 * c], csem.at[12], csem.at[13], (s, partner))
    agm.near(0)
    agm.across(1)
    agm.across(2)
    wait("wl")
    wait("wx")

    def fwd(i, _):
        tot = jnp.zeros((256, 1024), F32)
        for a in range(3):
            tot = tot + dot(s2o[pl.ds(4 * i + a, 4)].reshape(256, 1152), wv[9 * a : 9 * a + 9].reshape(1152, 1024))
        part[pl.ds(4 * i, 4)] = tot.astype(BF16).reshape(4, 64, 1024)
        return 0

    fwd(0, 0)
    agm.near(1)
    agm.near(2)
    agm.far(0)
    ring_relay(csl, xsem, 0)
    fwd(1, 0)
    agm.turn(1)
    agm.turn(2)
    to_owner(part, frecv, rsem)
    pend["part"] = lambda: owner_wait(frecv, rsem)
    got(cb.at[9 - 9 * c], csem.at[12], csem.at[13])
    if STOP == 3:
        pend["a"] = lambda: (ring_wait(csl, xsem, 0), agm.finish())
    stop(3)

    def back(i, _):
        tot = jnp.zeros((512, 384), F32)
        for a in range(3):
            rows = cb[2 - a : 10 - a].reshape(512, 1024)
            wt = wv[pl.ds(9 * a + 3 * i, 3)].reshape(384, 1024)
            tot = tot + lax.dot_general(rows, wt, (((1,), (1,)), ((), ())), preferred_element_type=F32)
        for j in range(3):
            acc[3 * i + j] = tot[:, 128 * j : 128 * j + 128]
        return 0

    lax.fori_loop(0, 3, back, 0)
    total = jnp.zeros((8, 64, 128), F32)
    for b in range(3):
        inner = jnp.zeros((8, 64, 128), F32)
        for cc in range(3):
            inner = inner + col_shift(acc[3 * b + cc].reshape(8, 64, 128), 2 - cc)
        total = total + row_shift(inner.reshape(512, 128), 2 - b).reshape(8, 64, 128)
    gm[...] = total.astype(BF16)
    to_owner(gm, grecv, gsem)
    pend["gm"] = lambda: owner_wait(grecv, gsem)

    ring_wait(csl, xsem, 0)
    agm.finish()
    stop(4)

    def wpart(t, ref):
        ct = jnp.transpose(csl[:, t].reshape(512, 128).astype(F32)).astype(BF16)
        for a in range(3):
            wacc[:, 1152 * a : 1152 * a + 1152] += dot(ct, ref[a : a + 8].reshape(512, 1152))

    wpart(s, s2o)

    def wgrad(i, _):
        t = ((zl + i // 4) % 2) * 4 + (s % 4 + 4 - i % 4) % 4
        taps10(mk[t], s2)
        wpart(t, s2)
        return 0

    lax.fori_loop(1, 8, wgrad, 0)
    stop(5)

    pcp = []
    for q, (lo, n) in enumerate(CHUNKS):
        for t in range(lo, lo + n):
            x = jnp.transpose(wacc[:, t * 128 : t * 128 + 128] * SCALE2)
            ownf[t] = jnp.where(c == 0, x[0:64], x[64:128])
            psend[t] = jnp.where(c == 0, x[64:128], x[0:64]).astype(BF16)
        cp = rcopy(psend.at[pl.ds(lo, n)], precv.at[pl.ds(lo, n)], psem.at[q], psem.at[7 + q], (s, partner))
        cp.start()
        pcp.append(cp)
    for q, (lo, n) in enumerate(CHUNKS):
        pcp[q].wait()
        gw[pl.ds(lo, n), :, pl.ds(pl.multiple_of(s * 128, 128), 128)] = (
            ownf[pl.ds(lo, n)] + precv[pl.ds(lo, n)].astype(F32)
        ).astype(BF16)
        agw.start(q)
    agw.start_z()
    if STOP == 6:
        agw.rest()
    stop(6)

    wait("gm")
    gpf = []
    for r in range(4):
        z = pre[r]
        th = gelu_parts(z)
        slope = 0.5 * (1.0 + th) + 0.5 * z * (1.0 - th * th) * ROOT * (1.0 + 3.0 * CUBIC * z * z)
        gpf.append(jnp.concatenate([grecv[2 * r], grecv[2 * r + 1]], axis=1).astype(F32) * slope)
    for j in range(8):
        rows = jnp.concatenate([gpf[r][8 * j : 8 * j + 8] for r in range(4)], axis=0)
        gpn[:, 256 * j : 256 * j + 256] = rows.astype(BF16)
    ghalo = [rcopy(gpn, gp, hsem.at[4], hsem.at[5], (s, up)), rcopy(gpn, gn, hsem.at[6], hsem.at[7], (s, down))]
    for h in ghalo:
        h.start()
    pend["ghalo"] = lambda: [h.wait() for h in ghalo]

    gx = jnp.concatenate([gpn[:, 256 * j : 256 * j + 256] for j in range(8)], axis=0)
    gt = jnp.transpose(gx.astype(F32)).astype(BF16)
    for ab in range(9):
        o = dot(gt, lhs[:, 512 * ab : 512 * ab + 512])
        even = o[0:64, 0:256] + o[128:192, 128:384]
        t = o[64:128, 128:384] + o[192:256, 256:512] + pltpu.roll(even, 192, 1)
        tbuf[64 * ab : 64 * ab + 64] = (t * SCALE1).astype(BF16)
    tbuf[576:640] = jnp.zeros((64, 256), BF16)
    lane = pl.ds(pl.multiple_of(c * 128, 128), 128)
    lane2 = pl.ds(pl.multiple_of(128 - c * 128, 128), 128)
    k1 = rcopy(tbuf.at[:, lane2], pbuf, ksem.at[0], ksem.at[1], (s, partner))
    k1.start()
    for q in XF:
        agw.near(q)
    k1.wait()
    own[...] = (tbuf[:, lane].astype(F32) + pbuf[...].astype(F32)).astype(BF16)
    k2s = []
    for i, (jz, jy) in enumerate(CHIPS):
        t = depth_peer(d, jz, jy, 0)
        k2s.append(rcopy(own.at[pl.ds(pl.multiple_of((t // 2) * 80, 16), 80)], rbuf.at[i], tsem.at[i], tsem.at[7 + i], (s, t)))
        k2s[-1].start()
    for q in ZF:
        agw.across(q)
    piece = pl.ds(pl.multiple_of(m * 80, 16), 80)
    tot = own[piece].astype(F32)
    for i in range(7):
        k2s[i].wait()
        tot = tot + rbuf[i].astype(F32)
    dbuf[7] = tot.astype(BF16)
    k3s = []
    for i, (jz, jx) in enumerate(SAMPS):
        k3s.append(rcopy(dbuf.at[7], dbuf.at[i], tsem.at[14 + i], tsem.at[21 + i], (sample_peer(s, jz, jx), d)))
        k3s[-1].start()
    if STOP == 7:
        for q in ZF:
            agw.near(q)
        for q in XF:
            agw.far(q)
        for q in ZF:
            agw.turn(q)
        agw.finish()
        for x in k3s:
            x.wait()
    stop(7)

    wait("ghalo")
    perms = [onehot((32, 32), lambda u, q, b=b: nat(q) == nat(u) + b - 1) for b in range(3)]
    perms[1] = None
    fill_rows(lhsb, edge_planes(gp[...], gpn[...], gn[...], d), perms)
    res = dot(lhsb[...], bandb[...]).astype(BF16)
    wide = jnp.concatenate([res[32 * j : 32 * j + 32] for j in range(8)], axis=1)
    gvol[...] = dot(onehot((32, 32), lambda i, q: nat(q) == i), wide).astype(BF16)
    for q in ZF:
        agw.near(q)
    for q in XF:
        agw.far(q)

    wait("part")
    tot = frecv[0].astype(F32)
    for i in range(1, 8):
        tot = tot + frecv[i].astype(F32)
    feat[...] = dot(perm64, tot.astype(BF16)).astype(BF16)
    for q in ZF:
        agw.turn(q)

    for x in k3s:
        x.wait()
    tot = None
    for j in range(8):
        idx = ((j // 4 + zl) % 2) * 4 + (s % 4 + 4 - j % 4) % 4
        idx = jnp.where(idx == 0, 7, idx - 1)
        val = dbuf[idx].astype(F32)
        tot = val if tot is None else tot + val
    own[piece] = tot.astype(BF16)
    k4s = []
    for i, (jz, jy) in enumerate(CHIPS):
        k4s.append(rcopy(own.at[piece], rbuf2.at[i], tsem.at[28 + i], tsem.at[35 + i], (s, depth_peer(d, jz, jy, 0))))
        k4s[-1].start()
    for i, (jz, jy) in enumerate(CHIPS):
        k4s[i].wait()
        own[pl.ds(pl.multiple_of((depth_src(d, jz, jy, 0) // 2) * 80, 16), 80)] = rbuf2[i]
    k5 = rcopy(own, pbuf2, ksem.at[2], ksem.at[3], (s, partner))
    k5.start()
    k5.wait()
    left = jnp.where(c == 0, own[...], pbuf2[...]).astype(F32)
    right = jnp.where(c == 0, pbuf2[...], own[...]).astype(F32)
    for ab in range(9):
        both = jnp.concatenate([left[64 * ab : 64 * ab + 64], right[64 * ab : 64 * ab + 64]], axis=1)
        o1[3 * ab : 3 * ab + 3] = jnp.transpose(both)[0:192].reshape(3, 64, 64)
    agw.finish()
    for cond, cp in late:
        wait_late(cond, cp)


def mega(v, cot, w1, w):
    dma = pltpu.SemaphoreType.DMA
    vm = lambda *shape: pltpu.VMEM(shape, BF16)
    vf = lambda *shape: pltpu.VMEM(shape, F32)
    scratch = [
        vm(32, 2048), vm(32, 2048), vm(64, 1024), vm(8, 64, 128), vm(10, 64, 1024), vm(8, 8, 64, 128),
        vm(27, 2, 64, 1024), vm(8, 10, 64, 128), vm(8, 64, 128), vm(256, 4608), vm(256, 4608), vm(4608, 256),
        vm(4608, 256), vm(10, 64, 1152), vm(10, 64, 1152), vm(8, 64, 1024), vm(8, 64, 1024),
        vm(8, 64, 128), vm(8, 64, 128), vf(9, 512, 128), vf(128, 3456), vf(4, 64, 256), vf(27, 64, 128),
        vm(27, 64, 128), vm(27, 64, 128), vm(32, 2048), vm(32, 2048), vm(32, 2048), vm(640, 256), vm(640, 128),
        vm(640, 128), vm(640, 128), vm(7, 80, 128), vm(8, 80, 128), vm(7, 80, 128),
        dma((3,)), dma((8,)), dma((14,)), dma((14,)), dma((14,)), dma((25,)), dma((21,)), dma((21,)), dma((16,)), dma((16,)),
        dma((14,)), dma((49,)), dma((49,)), dma((4,)), dma((42,)),
    ]
    return pl.pallas_call(
        mega_kernel,
        out_shape=[sds((64, 1024)), sds((32, 2048)), sds((27, 64, 64), F32), sds((27, 64, 1024))],
        in_specs=[VM, VM, VM, ANY],
        out_specs=[VM] * 4,
        scratch_shapes=scratch,
        compiler_params=pltpu.CompilerParams(vmem_limit_bytes=LIMIT, collective_id=1, has_side_effects=True),
        name="step",
    )(v, cot, w1, w)


def finish_kernel(gw, t, f, g, o2, o1, of, og):
    o2[...] = gw[...].astype(F32)

    @pl.when(pl.program_id(0) == 0)
    def _():
        of[...] = f[...]
        og[...] = g[...]
        o1[...] = t[...]


def finish(gw, t, f, g):
    whole = lambda *shape: pl.BlockSpec(shape, lambda i: (0,) * len(shape))
    return pl.pallas_call(
        finish_kernel,
        grid=(9,),
        out_shape=[sds((27, 64, 1024), F32), sds((27, 64, 64), F32), sds((64, 1024)), sds((32, 2048))],
        in_specs=[pl.BlockSpec((3, 64, 1024), lambda i: (i, 0, 0)), whole(27, 64, 64), whole(64, 1024), whole(32, 2048)],
        out_specs=[pl.BlockSpec((3, 64, 1024), lambda i: (i, 0, 0)), whole(27, 64, 64), whole(64, 1024), whole(32, 2048)],
        compiler_params=pltpu.CompilerParams(vmem_limit_bytes=LIMIT),
        name="finish",
    )(gw, t, f, g)


def on_device(volume, conv1_weight, conv2_weight, cotangent):
    feat, gvol, o1, gw = mega(volume.reshape(32, 2048), cotangent.reshape(64, 1024), conv1_weight, conv2_weight)
    o2, o1, feat, gvol = finish(gw, o1, feat, gvol)
    return feat.reshape(1, 1, 8, 8, 1024), gvol.reshape(1, 1, 32, 2048), o1, o2


def solution(mesh):
    return jax.shard_map(
        on_device,
        mesh=mesh,
        in_specs=(P("sample", "depth", None, None), P(), P(None, "depth", None), P("sample", "depth", None, None, None)),
        out_specs=(P("sample", "depth", None, None, None), P("sample", "depth", None, None), P(), P(None, "depth", None)),
        check_vma=False,
    )
```

```python
import functools
import math

import jax
import jax.numpy as jnp
from jax import lax
from jax.experimental import pallas as pl
from jax.experimental.pallas import tpu as pltpu
from jax.sharding import PartitionSpec as P

MESH = pl.DeviceIdType.MESH
F32 = jnp.float32
BF16 = jnp.bfloat16
ROOT = 0.7978845608028654
CUBIC = 0.044715
SCALE1 = 1.0 / math.sqrt(8 * 16 * 32 * 32)
SCALE2 = 1.0 / math.sqrt(8 * 16 * 8 * 8)
VM = pl.BlockSpec(memory_space=pltpu.VMEM)
ANY = pl.BlockSpec(memory_space=pl.ANY)
LIMIT = 60 * 1024 * 1024


def where_am_i():
    s = lax.axis_index("sample")
    d = lax.axis_index("depth")
    return s, d


def rcopy(src, dst, ss, rs, dev):
    return pltpu.make_async_remote_copy(
        src_ref=src, dst_ref=dst, send_sem=ss, recv_sem=rs, device_id=dev, device_id_type=MESH
    )


def depth_peer(d, jz, jy, jc):
    zh, y, c = d // 8, (d // 2) % 4, d % 2
    return ((zh + jz) % 2) * 8 + ((y + jy) % 4) * 2 + (c + jc) % 2


def depth_src(d, jz, jy, jc):
    zh, y, c = d // 8, (d // 2) % 4, d % 2
    return ((zh + jz) % 2) * 8 + ((y + 4 - jy) % 4) * 2 + (c + jc) % 2


def sample_peer(s, jz, jx):
    return ((s // 4 + jz) % 2) * 4 + (s % 4 + jx) % 4


def sample_src(s, jz, jx):
    return ((s // 4 + jz) % 2) * 4 + (s % 4 + 4 - jx) % 4


CHIPS = [(jz, jy) for jz in range(2) for jy in range(4) if (jz, jy) != (0, 0)]
SAMPS = [(jz, jx) for jz in range(2) for jx in range(4) if (jz, jx) != (0, 0)]


def barrier(devs):
    bar = pltpu.get_barrier_semaphore()
    for dev in devs:
        pl.semaphore_signal(bar, inc=1, device_id=dev, device_id_type=MESH)
    pl.semaphore_wait(bar, len(devs))


def onehot(shape, fn):
    row = lax.broadcasted_iota(jnp.int32, shape, 0)
    col = lax.broadcasted_iota(jnp.int32, shape, 1)
    return jnp.where(fn(row, col), 1.0, 0.0).astype(BF16)


def dot(a, b):
    return jnp.dot(a, b, preferred_element_type=F32)


def nat(rho):
    return 4 * (rho % 8) + rho // 8


def call(kern, outs, ins, scratch, name, cid=None, specs=None, out_specs=None, **kw):
    params = dict(vmem_limit_bytes=LIMIT)
    if cid is not None:
        params.update(collective_id=cid, has_side_effects=True)
    return pl.pallas_call(
        kern,
        out_shape=outs,
        in_specs=specs or [VM] * len(ins),
        out_specs=out_specs or [VM] * len(outs),
        scratch_shapes=scratch,
        compiler_params=pltpu.CompilerParams(**params),
        name=name,
    )(*ins)


def sds(shape, dtype=BF16):
    return jax.ShapeDtypeStruct(shape, dtype)


def depth_of(zh, y, c):
    return zh * 8 + y * 2 + c


def fill_rows(lhs, planes, perms):
    zero = jnp.zeros((32, 128), BF16)
    for a in range(3):
        for b in range(3):
            x = planes[a] if perms[b] is None else dot(perms[b], planes[a]).astype(BF16)
            xp = jnp.concatenate([zero, x, zero], axis=1)
            for j in range(8):
                lhs[pl.ds(j * 32, 32), pl.ds((3 * a + b) * 512, 512)] = xp[:, 256 * j : 256 * j + 512]


def edge_planes(prev, own, nxt, d):
    zero = jnp.zeros_like(own)
    return [jnp.where(d > 0, prev, zero), own, jnp.where(d < 15, nxt, zero)]


def gelu_parts(value):
    inner = ROOT * (value + CUBIC * value * value * value)
    return jnp.tanh(inner)


def row_shift(x, b):
    if b == 1:
        return x
    rows = x.shape[0]
    lane = lax.broadcasted_iota(jnp.int32, x.shape, 0) % 8
    if b == 0:
        return jnp.where(lane == 0, 0.0, pltpu.roll(x, 1, 0))
    return jnp.where(lane == 7, 0.0, pltpu.roll(x, rows - 1, 0))


def col_shift(x, c):
    if c == 1:
        return x
    zero = jnp.zeros((x.shape[0], 8, x.shape[2]), x.dtype)
    if c == 0:
        return jnp.concatenate([zero, x[:, :56]], axis=1)
    return jnp.concatenate([x[:, 8:], zero], axis=1)


def taps10(x, s2):
    n = x.shape[0]
    flat = x.astype(F32).reshape(n * 64, 128)
    for b in range(3):
        y = row_shift(flat, b).reshape(n, 64, 128)
        for c in range(3):
            s2[:, :, (3 * b + c) * 128 : (3 * b + c + 1) * 128] = col_shift(y, c).astype(BF16)


def put_band(band, ab, w3):
    zero = jnp.zeros((64, 64), BF16)
    left = jnp.concatenate([w3, zero], axis=0)
    right = jnp.concatenate([zero, w3], axis=0)
    both = jnp.concatenate([left, right], axis=1)
    band[pl.ds(ab * 512 + 64, 256), 0:128] = both
    band[pl.ds(ab * 512 + 192, 256), 128:256] = both


def fill_band(band, w1):
    band[...] = jnp.zeros_like(band)
    for ab in range(9):
        put_band(band, ab, w1[3 * ab : 3 * ab + 3].reshape(192, 64))


def fill_band_back(band, w1):
    band[...] = jnp.zeros_like(band)
    for ab in range(9):
        top = 3 * (8 - ab) + 2
        w3 = [jnp.transpose(w1[top - c].astype(F32)).astype(BF16) for c in range(3)]
        put_band(band, ab, jnp.concatenate(w3, axis=0))


STOP = None


class Done(Exception):
    pass


CHUNKS = [(4 * q, min(4, 27 - 4 * q)) for q in range(7)]
XF = (0, 1, 2)
ZF = (3, 4, 5, 6)


def mega_kernel(*refs):
    try:
        mega_body(*refs)
    except Done:
        pass


def mega_body(
    v, cot, w1, w,
    feat, gvol, o1, gw,
    vp, vn, cotp, mine, cb, csl, wv, mk, moved, lhs, lhsb, band, bandb, s2o, s2, part, zrecv, frecv,
    gm, grecv, acc, wacc, pre, ownf, psend, precv, gpn, gp, gn, tbuf, tall, rbuf, dbuf,
    wsem, hsem, asem, csem, xsem, msem, ssend, srecv, gsem, rsem, psem, nsend, nrecv, tsem,
):
    s, d = where_am_i()
    zh, y, c = d // 8, (d // 2) % 4, d % 2
    m = d // 2
    zl = s // 4
    up, down = (d + 1) % 16, (d + 15) % 16
    partner = depth_of(zh, y, 1 - c)
    yp, ym = depth_of(zh, (y + 1) % 4, c), depth_of(zh, (y + 3) % 4, c)
    late = []
    pend = {}

    def stop(k):
        if STOP == k:
            for fn in list(pend.values()):
                fn()
            for cond, cp in late:
                wait_late(cond, cp)
            raise Done

    def wait(k):
        pend.pop(k)()

    def wait_late(cond, cp):
        if cond is None:
            cp.wait_send()
        else:

            @pl.when(cond)
            def _():
                cp.wait_send()

    def go(src, dst, ss, rs, dev):
        cp = rcopy(src, dst, ss, rs, dev)
        cp.start()
        late.append((None, cp))

    def got(ref, ss, rs):
        rcopy(ref, ref, ss, rs, (s, partner)).wait_recv()

    def spread(src_of, dst, sems):
        k = d % 8
        for i, (jz, jy) in enumerate([(0, 0)] + CHIPS):
            t = depth_of((zh + jz) % 2, (y + jy) % 4, zh)
            if i:
                go(src_of(t // 2), dst(k + 1), sems.at[i], sems.at[16 + k], (s, t))
            else:
                cp = rcopy(src_of(t // 2), dst(k + 1), sems.at[i], sems.at[16 + k], (s, t))

                @pl.when(t != d)
                def _(cp=cp):
                    cp.start()

                late.append((t != d, cp))
        rim = (d == 7) | (d == 8)
        for i, (jz, jy) in enumerate(CHIPS):
            t = depth_of((zh + jz) % 2, (y + jy) % 4, 1 - zh)
            cp = rcopy(src_of(t // 2), dst(zh * 9), sems.at[8 + i], sems.at[24], (s, t))

            @pl.when(rim)
            def _(cp=cp):
                cp.start()

            late.append((rim, cp))

    def spread_wait(dst, sems):
        for k in range(8):

            @pl.when(8 * c + k != d)
            def _(k=k):
                got(dst(k + 1), sems.at[0], sems.at[16 + k])

        q = 9 - 9 * c

        @pl.when(8 - c != d)
        def _():
            got(dst(q), sems.at[0], sems.at[24])

    def home_send(src, buf, sems, edge):
        k = d % 8 + edge
        here, there = depth_of(zh, y, zh), depth_of(1 - zh, y, zh)
        go(src, buf.at[k], sems.at[1], sems.at[4 + c], (s, there))
        cp = rcopy(src, buf.at[k], sems.at[0], sems.at[4 + c], (s, here))

        @pl.when(c != zh)
        def _():
            cp.start()

        late.append((c != zh, cp))

        @pl.when(c == zh)
        def _():
            buf[k] = src[...]

    def home_wait(buf, sems, edge):
        for j in range(2):

            @pl.when((zh != c) | (c != j))
            def _(j=j):
                got(buf.at[2 * y + j + edge], sems.at[0], sems.at[4 + j])

    def ring_send(buf, sems, edge):
        two = buf.at[pl.ds(2 * y + edge, 2)]
        go(two, two, sems.at[2], sems.at[6], (s, yp))
        go(two, two, sems.at[3], sems.at[7], (s, ym))

    def ring_relay(buf, sems, edge):
        lo, hi = (y + 3) % 4, (y + 1) % 4
        got(buf.at[pl.ds(2 * lo + edge, 2)], sems.at[2], sems.at[6])
        one = buf.at[2 * lo + edge]
        go(one, one, sems.at[8], sems.at[10], (s, yp))
        got(buf.at[pl.ds(2 * hi + edge, 2)], sems.at[3], sems.at[7])
        one = buf.at[2 * hi + 1 + edge]
        go(one, one, sems.at[9], sems.at[11], (s, ym))

    def ring_wait(buf, sems, edge):
        far = (y + 2) % 4
        got(buf.at[2 * far + edge], sems.at[8], sems.at[10])
        got(buf.at[2 * far + 1 + edge], sems.at[9], sems.at[11])

    def features_z():
        cp = rcopy(part, zrecv, rsem.at[0], rsem.at[1], (s, depth_of(1 - zh, y, c)))

        @pl.when(zh != c)
        def _():
            cp.start()

        late.append((zh != c, cp))

    def features_y():
        cps = []
        for i in range(8):
            if i < 2:
                q, dev = 2 * y + i, depth_of(zh, y, i)
            else:
                q = 2 * ((y + i // 2) % 4) + i % 2
                dev = depth_of(zh, (y + i // 2) % 4, i % 2)
            cps.append((dev != d, rcopy(part.at[q], frecv.at[y], rsem.at[2 + i], rsem.at[10 + y], (s, dev))))

        @pl.when(zh == c)
        def _():
            got(zrecv, rsem.at[0], rsem.at[1])
            for i in range(8):
                part[i] = (part[i].astype(F32) + zrecv[i].astype(F32)).astype(BF16)
            for i, (cond, cp) in enumerate(cps):
                if i >= 2:
                    cp.start()
                else:

                    @pl.when(cond)
                    def _(cp=cp):
                        cp.start()

            frecv[y] = part[2 * y + c]

        for cond, cp in cps:
            late.append(((zh == c) & cond, cp))

    def features_wait():
        for j in range(4):

            @pl.when((j != y) | (zh != c))
            def _(j=j):
                got(frecv.at[j], rsem.at[0], rsem.at[10 + j])

    def to_owner(src, dst, sems, which=range(8)):
        for i in which:
            p = 8 * c + i
            cp = rcopy(src.at[i], dst.at[m], sems.at[i], sems.at[8 + m], (s, p))

            @pl.when(p != d)
            def _(cp=cp):
                cp.start()

            @pl.when(p == d)
            def _(i=i):
                dst[m] = src[i]

            late.append((p != d, cp))

    def owner_wait(dst, sems):
        for j in range(8):

            @pl.when(2 * j + zh != d)
            def _(j=j):
                got(dst.at[j], sems.at[0], sems.at[8 + j])

    xp, xm, x2 = sample_peer(s, 0, 1), sample_peer(s, 0, 3), sample_peer(s, 0, 2)
    zo, oxp, oxm, ox2 = sample_peer(s, 1, 0), sample_peer(s, 1, 1), sample_peer(s, 1, 3), sample_peer(s, 1, 2)

    class Gather:
        def __init__(self, ref, xf, zf, ss, rs):
            self.ref, self.xf, self.zf, self.ss, self.rs = ref, xf, zf, ss, rs

        def send(self, q, kind, block, dev):
            r = self.ref(block, q)
            go(r, r, self.ss.at[7 * q + kind], self.rs.at[7 * q + kind], (dev, d))

        def recv(self, q, kind, block):
            got(self.ref(block, q), self.ss.at[7 * q + kind], self.rs.at[7 * q + kind])

        def start(self, q):
            if q in self.zf:
                self.send(q, 0, s, zo)
            self.send(q, 1, s, xp)
            self.send(q, 2, s, xm)

        def start_z(self):
            for q in self.xf:
                self.send(q, 0, s, zo)

        def near(self, q):
            self.recv(q, 1, xm)
            if q % 2 == 0:
                self.send(q, 3, xm, xp)
            if q in self.xf:
                self.send(q, 4, xm, zo)
            self.recv(q, 2, xp)
            if q % 2:
                self.send(q, 3, xp, xm)
            if q in self.xf:
                self.send(q, 5, xp, zo)

        def across(self, q):
            self.recv(q, 0, zo)
            self.send(q, 4, zo, xp)
            self.send(q, 5, zo, xm)

        def far(self, q):
            self.recv(q, 3, x2)
            self.send(q, 6, x2, zo)

        def turn(self, q):
            self.recv(q, 4, oxm)
            if q % 2 == 0:
                self.send(q, 6, oxm, xp)
            self.recv(q, 5, oxp)
            if q % 2:
                self.send(q, 6, oxp, xm)

        def finish(self):
            for q in self.xf:
                self.recv(q, 0, zo)
                self.recv(q, 4, oxm)
                self.recv(q, 5, oxp)
                self.recv(q, 6, ox2)
            for q in self.zf:
                self.recv(q, 3, x2)
                self.recv(q, 6, ox2)

        def rest(self):
            for q in self.xf:
                self.near(q)
            for q in self.zf:
                self.across(q)
            for q in self.zf:
                self.near(q)
            for q in self.xf:
                self.far(q)
            for q in self.zf:
                self.turn(q)
            self.finish()

    agm = Gather(lambda b, q: mk.at[b, pl.ds(1 - c + 3 * q, 3)], (0,), (1, 2), ssend, srecv)
    agw = Gather(
        lambda b, q: gw.at[pl.ds(*CHUNKS[q]), :, pl.ds(pl.multiple_of(b * 128, 128), 128)], XF, ZF, nsend, nrecv
    )

    wl = pltpu.make_async_copy(w, wv.at[:, c], wsem.at[0])
    wl.start()
    pend["wl"] = wl.wait
    bar = pltpu.get_barrier_semaphore()
    friends = [
        (s, depth_peer(d, jz, jy, jc)) for jz in range(2) for jy in range(4) for jc in range(2) if (jz, jy, jc) != (0, 0, 0)
    ] + [(sample_peer(s, jz, jx), d) for jz, jx in SAMPS]
    for dev in friends:
        pl.semaphore_signal(bar, inc=1, device_id=dev, device_id_type=MESH)
    perm64 = onehot((64, 64), lambda u, q: q == (u % 8) * 8 + u // 8)
    cotp[...] = dot(perm64, cot[...]).astype(BF16)
    mine[s] = cotp[:, pl.ds(pl.multiple_of(s * 128, 128), 128)]
    cb[9 * c] = jnp.zeros((64, 1024), BF16)
    mk[:, 9 * c] = jnp.zeros((8, 64, 128), BF16)
    fill_band(band, w1)
    pl.semaphore_wait(bar, len(friends))
    stop(0)

    halo = [rcopy(v, vp, hsem.at[0], hsem.at[1], (s, up)), rcopy(v, vn, hsem.at[2], hsem.at[3], (s, down))]
    for h in halo:
        h.start()
    pend["halo"] = lambda: [h.wait() for h in halo]
    home_send(cotp, cb, csem, 1)
    for i, (jz, jx) in enumerate(SAMPS):
        t = sample_peer(s, jz, jx)
        go(cotp.at[:, pl.ds(pl.multiple_of(t * 128, 128), 128)], mine.at[s], asem.at[i], asem.at[7 + i], (t, d))
    wx = rcopy(w, wv.at[:, c], wsem.at[1], wsem.at[2], (s, partner))
    wx.start()
    pend["wx"] = wx.wait

    def mine_wait():
        for i, (jz, jx) in enumerate(SAMPS):
            got(mine.at[sample_src(s, jz, jx)], asem.at[i], asem.at[7 + i])

    pend["mine"] = mine_wait

    perms = [onehot((32, 32), lambda rho, i, b=b: i == nat(rho) + b - 1) for b in range(3)]
    wait("halo")
    fill_rows(lhs, edge_planes(vp[...], v[...], vn[...], d), perms)
    res = dot(lhs[...], band[...])
    for r in range(4):
        z = jnp.concatenate([res[j * 32 + r * 8 : j * 32 + r * 8 + 8] for j in range(8)], axis=0)
        pre[r] = z
        hid = (0.5 * z * (1.0 + gelu_parts(z))).astype(BF16)
        moved[2 * r] = hid[:, 0:128]
        moved[2 * r + 1] = hid[:, 128:256]
    spread(lambda t: moved.at[t], lambda k: mk.at[s, k], msem)
    pend["mk"] = lambda: spread_wait(lambda k: mk.at[s, k], msem)

    @pl.when(c == zh)
    def _():
        mk[s, d % 8 + 1] = moved[m]

    @pl.when((d == 7) | (d == 8))
    def _():
        mk[s, zh * 9] = moved[m]

    wait("mine")
    home_send(mine, csl, xsem, 0)
    fill_band_back(bandb, w1)
    wacc[...] = jnp.zeros_like(wacc)
    home_wait(csl, xsem, 0)
    ring_send(csl, xsem, 0)

    wait("mk")
    for q in range(3):
        agm.start(q)
    agm.start_z()
    if STOP == 1:
        pend["a"] = lambda: (ring_relay(csl, xsem, 0), home_wait(cb, csem, 1), ring_wait(csl, xsem, 0), agm.rest())
    stop(1)
    taps10(mk[s], s2o)
    wait("wl")
    wait("wx")

    def fwd(i):
        tot = jnp.zeros((256, 1024), F32)
        for a in range(3):
            tot = tot + dot(s2o[4 * i + a : 4 * i + a + 4].reshape(256, 1152), wv[9 * a : 9 * a + 9].reshape(1152, 1024))
        part[4 * i : 4 * i + 4] = tot.astype(BF16).reshape(4, 64, 1024)

    fwd(0)
    ring_relay(csl, xsem, 0)
    home_wait(cb, csem, 1)
    ring_send(cb, csem, 1)
    agm.near(0)
    agm.across(1)
    agm.across(2)
    fwd(1)
    agm.near(1)
    agm.near(2)
    agm.far(0)
    features_z()

    def fz():
        @pl.when(zh == c)
        def _():
            got(zrecv, rsem.at[0], rsem.at[1])

    pend["fz"] = fz
    ring_wait(csl, xsem, 0)

    def wpart(t, ref):
        ct = jnp.transpose(csl[:, t].reshape(512, 128).astype(F32)).astype(BF16)
        for a in range(3):
            wacc[:, 1152 * a : 1152 * a + 1152] += dot(ct, ref[a : a + 8].reshape(512, 1152))

    def wgrad(i, _):
        j = jnp.where(i == 2, 3, jnp.where(i == 3, 2, i))
        t = ((zl + j // 4) % 2) * 4 + (s % 4 + 4 - j % 4) % 4
        taps10(mk[t], s2)
        wpart(t, s2)
        return 0

    wpart(s, s2o)
    agm.turn(1)
    agm.turn(2)
    ring_relay(cb, csem, 1)
    lax.fori_loop(1, 3, wgrad, 0)
    if STOP == 2:
        pend["a"] = lambda: (agm.finish(), ring_wait(cb, csem, 1))
    stop(2)
    ring_wait(cb, csem, 1)
    go(cb.at[8 - 7 * c], cb.at[9 * c], csem.at[12], csem.at[13], (s, partner))
    agm.finish()
    lax.fori_loop(3, 5, wgrad, 0)
    got(cb.at[9 - 9 * c], csem.at[12], csem.at[13])
    stop(3)

    def back(i, _):
        tot = jnp.zeros((512, 384), F32)
        for a in range(3):
            rows = cb[2 - a : 10 - a].reshape(512, 1024)
            wt = wv[pl.ds(9 * a + 3 * i, 3)].reshape(384, 1024)
            tot = tot + lax.dot_general(rows, wt, (((1,), (1,)), ((), ())), preferred_element_type=F32)
        for j in range(3):
            acc[3 * i + j] = tot[:, 128 * j : 128 * j + 128]
        return 0

    lax.fori_loop(0, 3, back, 0)
    total = jnp.zeros((8, 64, 128), F32)
    for b in range(3):
        inner = jnp.zeros((8, 64, 128), F32)
        for cc in range(3):
            inner = inner + col_shift(acc[3 * b + cc].reshape(8, 64, 128), 2 - cc)
        total = total + row_shift(inner.reshape(512, 128), 2 - b).reshape(8, 64, 128)
    gm[...] = total.astype(BF16)
    to_owner(gm, grecv, gsem)
    pend["gm"] = lambda: owner_wait(grecv, gsem)
    lax.fori_loop(5, 8, wgrad, 0)
    if STOP == 8:
        pend.pop("fz")
        for q in range(0):
            pass
        pend["fz"] = fz
    stop(8)
    pend.pop("fz")
    features_y()
    pend["part"] = features_wait
    stop(4)

    pcp = []
    for q, (lo, n) in enumerate(CHUNKS):
        for t in range(lo, lo + n):
            x = jnp.transpose(wacc[:, t * 128 : t * 128 + 128] * SCALE2)
            ownf[t] = jnp.where(c == 0, x[0:64], x[64:128])
            psend[t] = jnp.where(c == 0, x[64:128], x[0:64]).astype(BF16)
        cp = rcopy(psend.at[pl.ds(lo, n)], precv.at[pl.ds(lo, n)], psem.at[q], psem.at[7 + q], (s, partner))
        cp.start()
        pcp.append(cp)
    for q, (lo, n) in enumerate(CHUNKS):
        pcp[q].wait()
        gw[pl.ds(lo, n), :, pl.ds(pl.multiple_of(s * 128, 128), 128)] = (
            ownf[pl.ds(lo, n)] + precv[pl.ds(lo, n)].astype(F32)
        ).astype(BF16)
        agw.start(q)
    agw.start_z()
    if STOP == 5:
        agw.rest()
    stop(5)

    wait("gm")
    gpf = []
    for r in range(4):
        z = pre[r]
        th = gelu_parts(z)
        slope = 0.5 * (1.0 + th) + 0.5 * z * (1.0 - th * th) * ROOT * (1.0 + 3.0 * CUBIC * z * z)
        gpf.append(jnp.concatenate([grecv[2 * r], grecv[2 * r + 1]], axis=1).astype(F32) * slope)
    for j in range(8):
        rows = jnp.concatenate([gpf[r][8 * j : 8 * j + 8] for r in range(4)], axis=0)
        gpn[:, 256 * j : 256 * j + 256] = rows.astype(BF16)
    ghalo = [rcopy(gpn, gp, hsem.at[4], hsem.at[5], (s, up)), rcopy(gpn, gn, hsem.at[6], hsem.at[7], (s, down))]
    for h in ghalo:
        h.start()
    pend["ghalo"] = lambda: [h.wait() for h in ghalo]

    gx = jnp.concatenate([gpn[:, 256 * j : 256 * j + 256] for j in range(8)], axis=0)
    gt = jnp.transpose(gx.astype(F32)).astype(BF16)
    for ab in range(9):
        o = dot(gt, lhs[:, 512 * ab : 512 * ab + 512])
        even = o[0:64, 0:256] + o[128:192, 128:384]
        t = o[64:128, 128:384] + o[192:256, 256:512] + pltpu.roll(even, 192, 1)
        tbuf[64 * ab : 64 * ab + 64] = (t * SCALE1).astype(BF16)
    tbuf[576:640] = jnp.zeros((64, 256), BF16)

    offs = [(jz, jy, jc) for jz in range(2) for jy in range(4) for jc in range(2) if (jz, jy, jc) != (0, 0, 0)]

    def piece(t):
        return pl.ds(pl.multiple_of((t // 2) * 80, 16), 80), pl.ds(pl.multiple_of((t % 2) * 128, 128), 128)

    k2s = []
    for i, o in enumerate(offs):
        t = depth_peer(d, *o)
        k2s.append(rcopy(tbuf.at[piece(t)], rbuf.at[i], tsem.at[i], tsem.at[15 + i], (s, t)))
        k2s[-1].start()
    for q in XF:
        agw.near(q)
    for q in ZF:
        agw.across(q)
    if STOP == 7:
        for q in ZF:
            agw.near(q)
        for q in XF:
            agw.far(q)
        for q in ZF:
            agw.turn(q)
        agw.finish()
        pend["k2"] = lambda: [x.wait() for x in k2s]
    stop(7)

    wait("part")
    tot = frecv[0].astype(F32)
    for i in range(1, 4):
        tot = tot + frecv[i].astype(F32)
    feat[...] = dot(perm64, tot.astype(BF16)).astype(BF16)

    wait("ghalo")
    perms = [onehot((32, 32), lambda u, q, b=b: nat(q) == nat(u) + b - 1) for b in range(3)]
    perms[1] = None
    fill_rows(lhsb, edge_planes(gp[...], gpn[...], gn[...], d), perms)
    tot = tbuf[piece(d)].astype(F32)
    for i in range(15):
        k2s[i].wait()
        tot = tot + rbuf[i].astype(F32)
    dbuf[7] = tot.astype(BF16)
    k3s = []
    for i, (jz, jx) in enumerate(SAMPS):
        k3s.append(rcopy(dbuf.at[7], dbuf.at[i], tsem.at[30 + i], tsem.at[37 + i], (sample_peer(s, jz, jx), d)))
        k3s[-1].start()
    for q in ZF:
        agw.near(q)
    res = dot(lhsb[...], bandb[...]).astype(BF16)
    wide = jnp.concatenate([res[32 * j : 32 * j + 32] for j in range(8)], axis=1)
    gvol[...] = dot(onehot((32, 32), lambda i, q: nat(q) == i), wide).astype(BF16)
    for q in XF:
        agw.far(q)
    if STOP == 9:
        for q in ZF:
            agw.turn(q)
        agw.finish()
        pend["k3"] = lambda: [x.wait() for x in k3s]
    stop(9)
    for q in ZF:
        agw.turn(q)
    for x in k3s:
        x.wait()
    tot = None
    for j in range(8):
        idx = ((j // 4 + zl) % 2) * 4 + (s % 4 + 4 - j % 4) % 4
        idx = jnp.where(idx == 0, 7, idx - 1)
        val = dbuf[idx].astype(F32)
        tot = val if tot is None else tot + val
    tall[piece(d)] = tot.astype(BF16)
    k4s = []
    for i, o in enumerate(offs):
        k4s.append(rcopy(tall.at[piece(d)], tall.at[piece(d)], tsem.at[44 + i], tsem.at[59 + i], (s, depth_peer(d, *o))))
        k4s[-1].start()

    for i, o in enumerate(offs):
        got(tall.at[piece(depth_src(d, *o))], tsem.at[44 + i], tsem.at[59 + i])
        k4s[i].wait_send()
    for ab in range(9):
        o1[3 * ab : 3 * ab + 3] = jnp.transpose(tall[64 * ab : 64 * ab + 64].astype(F32))[0:192].reshape(3, 64, 64)
    agw.finish()
    for cond, cp in late:
        wait_late(cond, cp)


def mega(v, cot, w1, w):
    dma = pltpu.SemaphoreType.DMA
    vm = lambda *shape: pltpu.VMEM(shape, BF16)
    vf = lambda *shape: pltpu.VMEM(shape, F32)
    scratch = [
        vm(32, 2048), vm(32, 2048), vm(64, 1024), vm(8, 64, 128), vm(10, 64, 1024), vm(8, 8, 64, 128),
        vm(27, 2, 64, 1024), vm(8, 10, 64, 128), vm(8, 64, 128), vm(256, 4608), vm(256, 4608), vm(4608, 256),
        vm(4608, 256), vm(10, 64, 1152), vm(10, 64, 1152), vm(8, 64, 1024), vm(8, 64, 1024), vm(4, 64, 1024),
        vm(8, 64, 128), vm(8, 64, 128), vf(9, 512, 128), vf(128, 3456), vf(4, 64, 256), vf(27, 64, 128),
        vm(27, 64, 128), vm(27, 64, 128), vm(32, 2048), vm(32, 2048), vm(32, 2048), vm(640, 256), vm(640, 256),
        vm(15, 80, 128), vm(8, 80, 128),
        dma((3,)), dma((8,)), dma((14,)), dma((14,)), dma((14,)), dma((25,)), dma((21,)), dma((21,)), dma((16,)), dma((16,)),
        dma((14,)), dma((49,)), dma((49,)), dma((74,)),
    ]
    return pl.pallas_call(
        mega_kernel,
        out_shape=[sds((64, 1024)), sds((32, 2048)), sds((27, 64, 64), F32), sds((27, 64, 1024))],
        in_specs=[VM, VM, VM, ANY],
        out_specs=[VM] * 4,
        scratch_shapes=scratch,
        compiler_params=pltpu.CompilerParams(vmem_limit_bytes=LIMIT, collective_id=1, has_side_effects=True),
        name="step",
    )(v, cot, w1, w)


def finish_kernel(gw, t, f, g, o2, o1, of, og, narrow, wide, tv, fv, gv, isem, osem):
    loads = [pltpu.make_async_copy(gw.at[pl.ds(3 * i, 3)], narrow.at[pl.ds(3 * i, 3)], isem.at[i]) for i in range(9)]
    small_in = [pltpu.make_async_copy(a, b, isem.at[9 + i]) for i, (a, b) in enumerate([(t, tv), (f, fv), (g, gv)])]
    stores = [pltpu.make_async_copy(wide.at[pl.ds(3 * i, 3)], o2.at[pl.ds(3 * i, 3)], osem.at[i]) for i in range(9)]
    small_out = [pltpu.make_async_copy(a, b, osem.at[9 + i]) for i, (a, b) in enumerate([(tv, o1), (fv, of), (gv, og)])]
    for x in loads + small_in:
        x.start()
    for i in range(9):
        loads[i].wait()
        wide[3 * i : 3 * i + 3] = narrow[3 * i : 3 * i + 3].astype(F32)
        stores[i].start()
    for a, b in zip(small_in, small_out):
        a.wait()
        b.start()
    for x in stores + small_out:
        x.wait()


def finish(gw, t, f, g):
    dma = pltpu.SemaphoreType.DMA
    return pl.pallas_call(
        finish_kernel,
        out_shape=[sds((27, 64, 1024), F32), sds((27, 64, 64), F32), sds((64, 1024)), sds((32, 2048))],
        in_specs=[ANY] * 4,
        out_specs=[ANY] * 4,
        scratch_shapes=[
            pltpu.VMEM((27, 64, 1024), BF16),
            pltpu.VMEM((27, 64, 1024), F32),
            pltpu.VMEM((27, 64, 64), F32),
            pltpu.VMEM((64, 1024), BF16),
            pltpu.VMEM((32, 2048), BF16),
            dma((12,)),
            dma((12,)),
        ],
        compiler_params=pltpu.CompilerParams(vmem_limit_bytes=LIMIT),
        name="finish",
    )(gw, t, f, g)


def on_device(volume, conv1_weight, conv2_weight, cotangent):
    feat, gvol, o1, gw = mega(volume.reshape(32, 2048), cotangent.reshape(64, 1024), conv1_weight, conv2_weight)
    o2, o1, feat, gvol = finish(gw, o1, feat, gvol)
    return feat.reshape(1, 1, 8, 8, 1024), gvol.reshape(1, 1, 32, 2048), o1, o2


def solution(mesh):
    return jax.shard_map(
        on_device,
        mesh=mesh,
        in_specs=(P("sample", "depth", None, None), P(), P(None, "depth", None), P("sample", "depth", None, None, None)),
        out_specs=(P("sample", "depth", None, None, None), P("sample", "depth", None, None), P(), P(None, "depth", None)),
        check_vma=False,
    )
```

```python
import functools
import math

import jax
import jax.numpy as jnp
from jax import lax
from jax.experimental import pallas as pl
from jax.experimental.pallas import tpu as pltpu
from jax.sharding import PartitionSpec as P

MESH = pl.DeviceIdType.MESH
F32 = jnp.float32
BF16 = jnp.bfloat16
ROOT = 0.7978845608028654
CUBIC = 0.044715
SCALE1 = 1.0 / math.sqrt(8 * 16 * 32 * 32)
SCALE2 = 1.0 / math.sqrt(8 * 16 * 8 * 8)
VM = pl.BlockSpec(memory_space=pltpu.VMEM)
ANY = pl.BlockSpec(memory_space=pl.ANY)
LIMIT = 60 * 1024 * 1024


def where_am_i():
    s = lax.axis_index("sample")
    d = lax.axis_index("depth")
    return s, d


def rcopy(src, dst, ss, rs, dev):
    return pltpu.make_async_remote_copy(
        src_ref=src, dst_ref=dst, send_sem=ss, recv_sem=rs, device_id=dev, device_id_type=MESH
    )


def depth_peer(d, jz, jy, jc):
    zh, y, c = d // 8, (d // 2) % 4, d % 2
    return ((zh + jz) % 2) * 8 + ((y + jy) % 4) * 2 + (c + jc) % 2


def depth_src(d, jz, jy, jc):
    zh, y, c = d // 8, (d // 2) % 4, d % 2
    return ((zh + jz) % 2) * 8 + ((y + 4 - jy) % 4) * 2 + (c + jc) % 2


def sample_peer(s, jz, jx):
    return ((s // 4 + jz) % 2) * 4 + (s % 4 + jx) % 4


def sample_src(s, jz, jx):
    return ((s // 4 + jz) % 2) * 4 + (s % 4 + 4 - jx) % 4


CHIPS = [(jz, jy) for jz in range(2) for jy in range(4) if (jz, jy) != (0, 0)]
SAMPS = [(jz, jx) for jz in range(2) for jx in range(4) if (jz, jx) != (0, 0)]


def barrier(devs):
    bar = pltpu.get_barrier_semaphore()
    for dev in devs:
        pl.semaphore_signal(bar, inc=1, device_id=dev, device_id_type=MESH)
    pl.semaphore_wait(bar, len(devs))


def onehot(shape, fn):
    row = lax.broadcasted_iota(jnp.int32, shape, 0)
    col = lax.broadcasted_iota(jnp.int32, shape, 1)
    return jnp.where(fn(row, col), 1.0, 0.0).astype(BF16)


def dot(a, b):
    return jnp.dot(a, b, preferred_element_type=F32)


def nat(rho):
    return 4 * (rho % 8) + rho // 8


def call(kern, outs, ins, scratch, name, cid=None, specs=None, out_specs=None, **kw):
    params = dict(vmem_limit_bytes=LIMIT)
    if cid is not None:
        params.update(collective_id=cid, has_side_effects=True)
    return pl.pallas_call(
        kern,
        out_shape=outs,
        in_specs=specs or [VM] * len(ins),
        out_specs=out_specs or [VM] * len(outs),
        scratch_shapes=scratch,
        compiler_params=pltpu.CompilerParams(**params),
        name=name,
    )(*ins)


def sds(shape, dtype=BF16):
    return jax.ShapeDtypeStruct(shape, dtype)


def depth_of(zh, y, c):
    return zh * 8 + y * 2 + c


def fill_rows(lhs, planes, perms):
    zero = jnp.zeros((32, 128), BF16)
    for a in range(3):
        for b in range(3):
            x = planes[a] if perms[b] is None else dot(perms[b], planes[a]).astype(BF16)
            xp = jnp.concatenate([zero, x, zero], axis=1)
            for j in range(8):
                lhs[pl.ds(j * 32, 32), pl.ds((3 * a + b) * 512, 512)] = xp[:, 256 * j : 256 * j + 512]


def edge_planes(prev, own, nxt, d):
    zero = jnp.zeros_like(own)
    return [jnp.where(d > 0, prev, zero), own, jnp.where(d < 15, nxt, zero)]


def gelu_parts(value):
    inner = ROOT * (value + CUBIC * value * value * value)
    return jnp.tanh(inner)


def row_shift(x, b):
    if b == 1:
        return x
    rows = x.shape[0]
    lane = lax.broadcasted_iota(jnp.int32, x.shape, 0) % 8
    if b == 0:
        return jnp.where(lane == 0, 0.0, pltpu.roll(x, 1, 0))
    return jnp.where(lane == 7, 0.0, pltpu.roll(x, rows - 1, 0))


def col_shift(x, c):
    if c == 1:
        return x
    zero = jnp.zeros((x.shape[0], 8, x.shape[2]), x.dtype)
    if c == 0:
        return jnp.concatenate([zero, x[:, :56]], axis=1)
    return jnp.concatenate([x[:, 8:], zero], axis=1)


def taps10(x, s2):
    n = x.shape[0]
    flat = x.astype(F32).reshape(n * 64, 128)
    for b in range(3):
        y = row_shift(flat, b).reshape(n, 64, 128)
        for c in range(3):
            s2[:, :, (3 * b + c) * 128 : (3 * b + c + 1) * 128] = col_shift(y, c).astype(BF16)


def put_band(band, ab, w3):
    zero = jnp.zeros((64, 64), BF16)
    left = jnp.concatenate([w3, zero], axis=0)
    right = jnp.concatenate([zero, w3], axis=0)
    both = jnp.concatenate([left, right], axis=1)
    band[pl.ds(ab * 512 + 64, 256), 0:128] = both
    band[pl.ds(ab * 512 + 192, 256), 128:256] = both


def fill_band(band, w1):
    band[...] = jnp.zeros_like(band)
    for ab in range(9):
        put_band(band, ab, w1[3 * ab : 3 * ab + 3].reshape(192, 64))


def fill_band_back(band, w1):
    band[...] = jnp.zeros_like(band)
    for ab in range(9):
        top = 3 * (8 - ab) + 2
        w3 = [jnp.transpose(w1[top - c].astype(F32)).astype(BF16) for c in range(3)]
        put_band(band, ab, jnp.concatenate(w3, axis=0))


STOP = None


class Done(Exception):
    pass


CHUNKS = [(4 * q, min(4, 27 - 4 * q)) for q in range(7)]
XF = (0, 1, 2)
ZF = (3, 4, 5, 6)


def mega_kernel(*refs):
    try:
        mega_body(*refs)
    except Done:
        pass


def mega_body(
    v, cot, w1, w,
    feat, gvol, o1, gw,
    vp, vn, cotp, mine, cb, csl, wv, mk, moved, lhs, lhsb, band, bandb, s2o, s2, part, zrecv, frecv,
    gm, grecv, acc, wacc, pre, ownf, psend, precv, gpn, gp, gn, tbuf, tall, rbuf, dbuf,
    wsem, hsem, asem, csem, xsem, msem, ssend, srecv, gsem, rsem, psem, nsend, nrecv, tsem,
):
    s, d = where_am_i()
    zh, y, c = d // 8, (d // 2) % 4, d % 2
    m = d // 2
    zl = s // 4
    up, down = (d + 1) % 16, (d + 15) % 16
    partner = depth_of(zh, y, 1 - c)
    yp, ym = depth_of(zh, (y + 1) % 4, c), depth_of(zh, (y + 3) % 4, c)
    late = []
    pend = {}

    def stop(k):
        if STOP == k:
            for fn in list(pend.values()):
                fn()
            for cond, cp in late:
                wait_late(cond, cp)
            raise Done

    def wait(k):
        pend.pop(k)()

    def wait_late(cond, cp):
        if cond is None:
            cp.wait_send()
        else:

            @pl.when(cond)
            def _():
                cp.wait_send()

    def go(src, dst, ss, rs, dev):
        cp = rcopy(src, dst, ss, rs, dev)
        cp.start()
        late.append((None, cp))

    def got(ref, ss, rs):
        rcopy(ref, ref, ss, rs, (s, partner)).wait_recv()

    def spread(src_of, dst, sems):
        k = d % 8
        for i, (jz, jy) in enumerate([(0, 0)] + CHIPS):
            t = depth_of((zh + jz) % 2, (y + jy) % 4, zh)
            if i:
                go(src_of(t // 2), dst(k + 1), sems.at[i], sems.at[16 + k], (s, t))
            else:
                cp = rcopy(src_of(t // 2), dst(k + 1), sems.at[i], sems.at[16 + k], (s, t))

                @pl.when(t != d)
                def _(cp=cp):
                    cp.start()

                late.append((t != d, cp))
        rim = (d == 7) | (d == 8)
        for i, (jz, jy) in enumerate(CHIPS):
            t = depth_of((zh + jz) % 2, (y + jy) % 4, 1 - zh)
            cp = rcopy(src_of(t // 2), dst(zh * 9), sems.at[8 + i], sems.at[24], (s, t))

            @pl.when(rim)
            def _(cp=cp):
                cp.start()

            late.append((rim, cp))

    def spread_wait(dst, sems):
        for k in range(8):

            @pl.when(8 * c + k != d)
            def _(k=k):
                got(dst(k + 1), sems.at[0], sems.at[16 + k])

        q = 9 - 9 * c

        @pl.when(8 - c != d)
        def _():
            got(dst(q), sems.at[0], sems.at[24])

    def home_send(src, buf, sems, edge):
        k = d % 8 + edge
        here, there = depth_of(zh, y, zh), depth_of(1 - zh, y, zh)
        go(src, buf.at[k], sems.at[1], sems.at[4 + c], (s, there))
        cp = rcopy(src, buf.at[k], sems.at[0], sems.at[4 + c], (s, here))

        @pl.when(c != zh)
        def _():
            cp.start()

        late.append((c != zh, cp))

        @pl.when(c == zh)
        def _():
            buf[k] = src[...]

    def home_wait(buf, sems, edge):
        for j in range(2):

            @pl.when((zh != c) | (c != j))
            def _(j=j):
                got(buf.at[2 * y + j + edge], sems.at[0], sems.at[4 + j])

    def ring_send(buf, sems, edge):
        two = buf.at[pl.ds(2 * y + edge, 2)]
        go(two, two, sems.at[2], sems.at[6], (s, yp))
        go(two, two, sems.at[3], sems.at[7], (s, ym))

    def ring_relay(buf, sems, edge):
        lo, hi = (y + 3) % 4, (y + 1) % 4
        got(buf.at[pl.ds(2 * lo + edge, 2)], sems.at[2], sems.at[6])
        one = buf.at[2 * lo + edge]
        go(one, one, sems.at[8], sems.at[10], (s, yp))
        got(buf.at[pl.ds(2 * hi + edge, 2)], sems.at[3], sems.at[7])
        one = buf.at[2 * hi + 1 + edge]
        go(one, one, sems.at[9], sems.at[11], (s, ym))

    def ring_wait(buf, sems, edge):
        far = (y + 2) % 4
        got(buf.at[2 * far + edge], sems.at[8], sems.at[10])
        got(buf.at[2 * far + 1 + edge], sems.at[9], sems.at[11])

    def features_z():
        cp = rcopy(part, zrecv, rsem.at[0], rsem.at[1], (s, depth_of(1 - zh, y, c)))

        @pl.when(zh != c)
        def _():
            cp.start()

        late.append((zh != c, cp))

    def features_y():
        cps = []
        for i in range(8):
            if i < 2:
                q, dev = 2 * y + i, depth_of(zh, y, i)
            else:
                q = 2 * ((y + i // 2) % 4) + i % 2
                dev = depth_of(zh, (y + i // 2) % 4, i % 2)
            cps.append((dev != d, rcopy(part.at[q], frecv.at[y], rsem.at[2 + i], rsem.at[10 + y], (s, dev))))

        @pl.when(zh == c)
        def _():
            got(zrecv, rsem.at[0], rsem.at[1])
            for i in range(8):
                part[i] = (part[i].astype(F32) + zrecv[i].astype(F32)).astype(BF16)
            for i, (cond, cp) in enumerate(cps):
                if i >= 2:
                    cp.start()
                else:

                    @pl.when(cond)
                    def _(cp=cp):
                        cp.start()

            frecv[y] = part[2 * y + c]

        for cond, cp in cps:
            late.append(((zh == c) & cond, cp))

    def features_wait():
        for j in range(4):

            @pl.when((j != y) | (zh != c))
            def _(j=j):
                got(frecv.at[j], rsem.at[0], rsem.at[10 + j])

    def to_owner(src, dst, sems, which=range(8)):
        for i in which:
            p = 8 * c + i
            cp = rcopy(src.at[i], dst.at[m], sems.at[i], sems.at[8 + m], (s, p))

            @pl.when(p != d)
            def _(cp=cp):
                cp.start()

            @pl.when(p == d)
            def _(i=i):
                dst[m] = src[i]

            late.append((p != d, cp))

    def owner_wait(dst, sems):
        for j in range(8):

            @pl.when(2 * j + zh != d)
            def _(j=j):
                got(dst.at[j], sems.at[0], sems.at[8 + j])

    xp, xm, x2 = sample_peer(s, 0, 1), sample_peer(s, 0, 3), sample_peer(s, 0, 2)
    zo, oxp, oxm, ox2 = sample_peer(s, 1, 0), sample_peer(s, 1, 1), sample_peer(s, 1, 3), sample_peer(s, 1, 2)

    class Gather:
        def __init__(self, ref, xf, zf, ss, rs):
            self.ref, self.xf, self.zf, self.ss, self.rs = ref, xf, zf, ss, rs

        def send(self, q, kind, block, dev):
            r = self.ref(block, q)
            go(r, r, self.ss.at[7 * q + kind], self.rs.at[7 * q + kind], (dev, d))

        def recv(self, q, kind, block):
            got(self.ref(block, q), self.ss.at[7 * q + kind], self.rs.at[7 * q + kind])

        def start(self, q):
            if q in self.zf:
                self.send(q, 0, s, zo)
            self.send(q, 1, s, xp)
            self.send(q, 2, s, xm)

        def start_z(self):
            for q in self.xf:
                self.send(q, 0, s, zo)

        def near(self, q):
            self.recv(q, 1, xm)
            if q % 2 == 0:
                self.send(q, 3, xm, xp)
            if q in self.xf:
                self.send(q, 4, xm, zo)
            self.recv(q, 2, xp)
            if q % 2:
                self.send(q, 3, xp, xm)
            if q in self.xf:
                self.send(q, 5, xp, zo)

        def across(self, q):
            self.recv(q, 0, zo)
            self.send(q, 4, zo, xp)
            self.send(q, 5, zo, xm)

        def far(self, q):
            self.recv(q, 3, x2)
            self.send(q, 6, x2, zo)

        def turn(self, q):
            self.recv(q, 4, oxm)
            if q % 2 == 0:
                self.send(q, 6, oxm, xp)
            self.recv(q, 5, oxp)
            if q % 2:
                self.send(q, 6, oxp, xm)

        def finish(self):
            for q in self.xf:
                self.recv(q, 0, zo)
                self.recv(q, 4, oxm)
                self.recv(q, 5, oxp)
                self.recv(q, 6, ox2)
            for q in self.zf:
                self.recv(q, 3, x2)
                self.recv(q, 6, ox2)

        def rest(self):
            for q in self.xf:
                self.near(q)
            for q in self.zf:
                self.across(q)
            for q in self.zf:
                self.near(q)
            for q in self.xf:
                self.far(q)
            for q in self.zf:
                self.turn(q)
            self.finish()

    agm = Gather(lambda b, q: mk.at[b, pl.ds(1 - c + 3 * q, 3)], (0,), (1, 2), ssend, srecv)
    agw = Gather(
        lambda b, q: gw.at[pl.ds(*CHUNKS[q]), :, pl.ds(pl.multiple_of(b * 128, 128), 128)], XF, ZF, nsend, nrecv
    )

    wl = pltpu.make_async_copy(w, wv.at[:, c], wsem.at[0])
    wl.start()
    pend["wl"] = wl.wait
    bar = pltpu.get_barrier_semaphore()
    friends = [
        (s, depth_peer(d, jz, jy, jc)) for jz in range(2) for jy in range(4) for jc in range(2) if (jz, jy, jc) != (0, 0, 0)
    ] + [(sample_peer(s, jz, jx), d) for jz, jx in SAMPS]
    for dev in friends:
        pl.semaphore_signal(bar, inc=1, device_id=dev, device_id_type=MESH)
    perm64 = onehot((64, 64), lambda u, q: q == (u % 8) * 8 + u // 8)
    cotp[...] = dot(perm64, cot[...]).astype(BF16)
    mine[s] = cotp[:, pl.ds(pl.multiple_of(s * 128, 128), 128)]
    cb[9 * c] = jnp.zeros((64, 1024), BF16)
    mk[:, 9 * c] = jnp.zeros((8, 64, 128), BF16)
    fill_band(band, w1)
    pl.semaphore_wait(bar, len(friends))
    stop(0)

    halo = [rcopy(v, vp, hsem.at[0], hsem.at[1], (s, up)), rcopy(v, vn, hsem.at[2], hsem.at[3], (s, down))]
    for h in halo:
        h.start()
    pend["halo"] = lambda: [h.wait() for h in halo]
    home_send(cotp, cb, csem, 1)
    for i, (jz, jx) in enumerate(SAMPS):
        t = sample_peer(s, jz, jx)
        go(cotp.at[:, pl.ds(pl.multiple_of(t * 128, 128), 128)], mine.at[s], asem.at[i], asem.at[7 + i], (t, d))
    wx = rcopy(w, wv.at[:, c], wsem.at[1], wsem.at[2], (s, partner))
    wx.start()
    pend["wx"] = wx.wait

    def mine_wait():
        for i, (jz, jx) in enumerate(SAMPS):
            got(mine.at[sample_src(s, jz, jx)], asem.at[i], asem.at[7 + i])

    pend["mine"] = mine_wait

    perms = [onehot((32, 32), lambda rho, i, b=b: i == nat(rho) + b - 1) for b in range(3)]
    wait("halo")
    fill_rows(lhs, edge_planes(vp[...], v[...], vn[...], d), perms)
    res = dot(lhs[...], band[...])
    for r in range(4):
        z = jnp.concatenate([res[j * 32 + r * 8 : j * 32 + r * 8 + 8] for j in range(8)], axis=0)
        pre[r] = z
        hid = (0.5 * z * (1.0 + gelu_parts(z))).astype(BF16)
        moved[2 * r] = hid[:, 0:128]
        moved[2 * r + 1] = hid[:, 128:256]
    spread(lambda t: moved.at[t], lambda k: mk.at[s, k], msem)
    pend["mk"] = lambda: spread_wait(lambda k: mk.at[s, k], msem)

    @pl.when(c == zh)
    def _():
        mk[s, d % 8 + 1] = moved[m]

    @pl.when((d == 7) | (d == 8))
    def _():
        mk[s, zh * 9] = moved[m]

    wait("mine")
    home_send(mine, csl, xsem, 0)
    fill_band_back(bandb, w1)
    wacc[...] = jnp.zeros_like(wacc)
    home_wait(csl, xsem, 0)
    ring_send(csl, xsem, 0)

    wait("mk")
    for q in range(3):
        agm.start(q)
    agm.start_z()
    if STOP == 1:
        pend["a"] = lambda: (ring_relay(csl, xsem, 0), home_wait(cb, csem, 1), ring_wait(csl, xsem, 0), agm.rest())
    stop(1)
    taps10(mk[s], s2o)
    wait("wl")
    wait("wx")

    def fwd(i):
        tot = jnp.zeros((256, 1024), F32)
        for a in range(3):
            tot = tot + dot(s2o[4 * i + a : 4 * i + a + 4].reshape(256, 1152), wv[9 * a : 9 * a + 9].reshape(1152, 1024))
        part[4 * i : 4 * i + 4] = tot.astype(BF16).reshape(4, 64, 1024)

    fwd(0)
    ring_relay(csl, xsem, 0)
    home_wait(cb, csem, 1)
    ring_send(cb, csem, 1)
    agm.near(0)
    agm.across(1)
    agm.across(2)
    fwd(1)
    agm.near(1)
    agm.near(2)
    agm.far(0)
    features_z()

    def fz():
        @pl.when(zh == c)
        def _():
            got(zrecv, rsem.at[0], rsem.at[1])

    pend["fz"] = fz
    ring_wait(csl, xsem, 0)

    def wpart(t, ref):
        ct = jnp.transpose(csl[:, t].reshape(512, 128).astype(F32)).astype(BF16)
        for a in range(3):
            wacc[:, 1152 * a : 1152 * a + 1152] += dot(ct, ref[a : a + 8].reshape(512, 1152))

    def wgrad(i, _):
        j = jnp.where(i == 2, 3, jnp.where(i == 3, 2, i))
        t = ((zl + j // 4) % 2) * 4 + (s % 4 + 4 - j % 4) % 4
        taps10(mk[t], s2)
        wpart(t, s2)
        return 0

    wpart(s, s2o)
    agm.turn(1)
    agm.turn(2)
    ring_relay(cb, csem, 1)
    lax.fori_loop(1, 3, wgrad, 0)
    if STOP == 2:
        pend["a"] = lambda: (agm.finish(), ring_wait(cb, csem, 1))
    stop(2)
    ring_wait(cb, csem, 1)
    go(cb.at[8 - 7 * c], cb.at[9 * c], csem.at[12], csem.at[13], (s, partner))
    agm.finish()
    lax.fori_loop(3, 5, wgrad, 0)
    got(cb.at[9 - 9 * c], csem.at[12], csem.at[13])
    stop(3)

    def back(i, _):
        tot = jnp.zeros((512, 384), F32)
        for a in range(3):
            rows = cb[2 - a : 10 - a].reshape(512, 1024)
            wt = wv[pl.ds(9 * a + 3 * i, 3)].reshape(384, 1024)
            tot = tot + lax.dot_general(rows, wt, (((1,), (1,)), ((), ())), preferred_element_type=F32)
        for j in range(3):
            acc[3 * i + j] = tot[:, 128 * j : 128 * j + 128]
        return 0

    lax.fori_loop(0, 3, back, 0)
    total = jnp.zeros((8, 64, 128), F32)
    for b in range(3):
        inner = jnp.zeros((8, 64, 128), F32)
        for cc in range(3):
            inner = inner + col_shift(acc[3 * b + cc].reshape(8, 64, 128), 2 - cc)
        total = total + row_shift(inner.reshape(512, 128), 2 - b).reshape(8, 64, 128)
    gm[...] = total.astype(BF16)
    to_owner(gm, grecv, gsem)
    pend["gm"] = lambda: owner_wait(grecv, gsem)
    lax.fori_loop(5, 8, wgrad, 0)
    if STOP == 8:
        pend.pop("fz")
        for q in range(0):
            pass
        pend["fz"] = fz
    stop(8)
    pend.pop("fz")
    features_y()
    pend["part"] = features_wait
    stop(4)

    pcp = []
    for q, (lo, n) in enumerate(CHUNKS):
        for t in range(lo, lo + n):
            x = jnp.transpose(wacc[:, t * 128 : t * 128 + 128] * SCALE2)
            ownf[t] = jnp.where(c == 0, x[0:64], x[64:128])
            psend[t] = jnp.where(c == 0, x[64:128], x[0:64]).astype(BF16)
        cp = rcopy(psend.at[pl.ds(lo, n)], precv.at[pl.ds(lo, n)], psem.at[q], psem.at[7 + q], (s, partner))
        cp.start()
        pcp.append(cp)
    for q, (lo, n) in enumerate(CHUNKS):
        pcp[q].wait()
        gw[pl.ds(lo, n), :, pl.ds(pl.multiple_of(s * 128, 128), 128)] = (
            ownf[pl.ds(lo, n)] + precv[pl.ds(lo, n)].astype(F32)
        ).astype(BF16)
        agw.start(q)
    agw.start_z()
    if STOP == 5:
        agw.rest()
    stop(5)

    wait("gm")
    gpf = []
    for r in range(4):
        z = pre[r]
        th = gelu_parts(z)
        slope = 0.5 * (1.0 + th) + 0.5 * z * (1.0 - th * th) * ROOT * (1.0 + 3.0 * CUBIC * z * z)
        gpf.append(jnp.concatenate([grecv[2 * r], grecv[2 * r + 1]], axis=1).astype(F32) * slope)
    for j in range(8):
        rows = jnp.concatenate([gpf[r][8 * j : 8 * j + 8] for r in range(4)], axis=0)
        gpn[:, 256 * j : 256 * j + 256] = rows.astype(BF16)
    ghalo = [rcopy(gpn, gp, hsem.at[4], hsem.at[5], (s, up)), rcopy(gpn, gn, hsem.at[6], hsem.at[7], (s, down))]
    for h in ghalo:
        h.start()
    pend["ghalo"] = lambda: [h.wait() for h in ghalo]

    gx = jnp.concatenate([gpn[:, 256 * j : 256 * j + 256] for j in range(8)], axis=0)
    gt = jnp.transpose(gx.astype(F32)).astype(BF16)
    for ab in range(9):
        o = dot(gt, lhs[:, 512 * ab : 512 * ab + 512])
        even = o[0:64, 0:256] + o[128:192, 128:384]
        t = o[64:128, 128:384] + o[192:256, 256:512] + pltpu.roll(even, 192, 1)
        tbuf[64 * ab : 64 * ab + 64] = (t * SCALE1).astype(BF16)
    tbuf[576:640] = jnp.zeros((64, 256), BF16)

    offs = [(jz, jy, jc) for jz in range(2) for jy in range(4) for jc in range(2) if (jz, jy, jc) != (0, 0, 0)]

    def piece(t):
        return pl.ds(pl.multiple_of((t // 2) * 80, 16), 80), pl.ds(pl.multiple_of((t % 2) * 128, 128), 128)

    k2s = []
    for i, o in enumerate(offs):
        t = depth_peer(d, *o)
        k2s.append(rcopy(tbuf.at[piece(t)], rbuf.at[i], tsem.at[i], tsem.at[15 + i], (s, t)))
        k2s[-1].start()
    for q in XF:
        agw.near(q)
    for q in ZF:
        agw.across(q)
    if STOP == 7:
        for q in ZF:
            agw.near(q)
        for q in XF:
            agw.far(q)
        for q in ZF:
            agw.turn(q)
        agw.finish()
        pend["k2"] = lambda: [x.wait() for x in k2s]
    stop(7)

    wait("part")
    tot = frecv[0].astype(F32)
    for i in range(1, 4):
        tot = tot + frecv[i].astype(F32)
    feat[...] = dot(perm64, tot.astype(BF16)).astype(BF16)

    wait("ghalo")
    perms = [onehot((32, 32), lambda u, q, b=b: nat(q) == nat(u) + b - 1) for b in range(3)]
    perms[1] = None
    fill_rows(lhsb, edge_planes(gp[...], gpn[...], gn[...], d), perms)
    tot = tbuf[piece(d)].astype(F32)
    for i in range(15):
        k2s[i].wait()
        tot = tot + rbuf[i].astype(F32)
    dbuf[7] = tot.astype(BF16)
    k3s = []
    for i, (jz, jx) in enumerate(SAMPS):
        k3s.append(rcopy(dbuf.at[7], dbuf.at[i], tsem.at[30 + i], tsem.at[37 + i], (sample_peer(s, jz, jx), d)))
        k3s[-1].start()
    for q in ZF:
        agw.near(q)
    res = dot(lhsb[...], bandb[...]).astype(BF16)
    wide = jnp.concatenate([res[32 * j : 32 * j + 32] for j in range(8)], axis=1)
    gvol[...] = dot(onehot((32, 32), lambda i, q: nat(q) == i), wide).astype(BF16)
    for q in XF:
        agw.far(q)
    if STOP == 9:
        for q in ZF:
            agw.turn(q)
        agw.finish()
        pend["k3"] = lambda: [x.wait() for x in k3s]
    stop(9)
    for q in ZF:
        agw.turn(q)
    for x in k3s:
        x.wait()
    tot = None
    for j in range(8):
        idx = ((j // 4 + zl) % 2) * 4 + (s % 4 + 4 - j % 4) % 4
        idx = jnp.where(idx == 0, 7, idx - 1)
        val = dbuf[idx].astype(F32)
        tot = val if tot is None else tot + val
    tall[piece(d)] = tot.astype(BF16)
    k4s = []
    for i, o in enumerate(offs):
        k4s.append(rcopy(tall.at[piece(d)], tall.at[piece(d)], tsem.at[44 + i], tsem.at[59 + i], (s, depth_peer(d, *o))))
        k4s[-1].start()

    for i, o in enumerate(offs):
        got(tall.at[piece(depth_src(d, *o))], tsem.at[44 + i], tsem.at[59 + i])
        k4s[i].wait_send()
    for ab in range(9):
        o1[3 * ab : 3 * ab + 3] = jnp.transpose(tall[64 * ab : 64 * ab + 64].astype(F32))[0:192].reshape(3, 64, 64)
    agw.finish()
    for cond, cp in late:
        wait_late(cond, cp)


def mega(v, cot, w1, w):
    dma = pltpu.SemaphoreType.DMA
    vm = lambda *shape: pltpu.VMEM(shape, BF16)
    vf = lambda *shape: pltpu.VMEM(shape, F32)
    scratch = [
        vm(32, 2048), vm(32, 2048), vm(64, 1024), vm(8, 64, 128), vm(10, 64, 1024), vm(8, 8, 64, 128),
        vm(27, 2, 64, 1024), vm(8, 10, 64, 128), vm(8, 64, 128), vm(256, 4608), vm(256, 4608), vm(4608, 256),
        vm(4608, 256), vm(10, 64, 1152), vm(10, 64, 1152), vm(8, 64, 1024), vm(8, 64, 1024), vm(4, 64, 1024),
        vm(8, 64, 128), vm(8, 64, 128), vf(9, 512, 128), vf(128, 3456), vf(4, 64, 256), vf(27, 64, 128),
        vm(27, 64, 128), vm(27, 64, 128), vm(32, 2048), vm(32, 2048), vm(32, 2048), vm(640, 256), vm(640, 256),
        vm(15, 80, 128), vm(8, 80, 128),
        dma((3,)), dma((8,)), dma((14,)), dma((14,)), dma((14,)), dma((25,)), dma((21,)), dma((21,)), dma((16,)), dma((16,)),
        dma((14,)), dma((49,)), dma((49,)), dma((74,)),
    ]
    return pl.pallas_call(
        mega_kernel,
        out_shape=[sds((64, 1024)), sds((32, 2048)), sds((27, 64, 64), F32), sds((27, 64, 1024))],
        in_specs=[VM, VM, VM, ANY],
        out_specs=[VM] * 4,
        scratch_shapes=scratch,
        compiler_params=pltpu.CompilerParams(vmem_limit_bytes=46 * 1024 * 1024, collective_id=1, has_side_effects=True),
        name="step",
    )(v, cot, w1, w)


def finish_kernel(gw, t, f, g, o2, o1, of, og, narrow, wide, tv, fv, gv, isem, osem):
    loads = [pltpu.make_async_copy(gw.at[pl.ds(3 * i, 3)], narrow.at[pl.ds(3 * i, 3)], isem.at[i]) for i in range(9)]
    small_in = [pltpu.make_async_copy(a, b, isem.at[9 + i]) for i, (a, b) in enumerate([(t, tv), (f, fv), (g, gv)])]
    stores = [pltpu.make_async_copy(wide.at[pl.ds(3 * i, 3)], o2.at[pl.ds(3 * i, 3)], osem.at[i]) for i in range(9)]
    small_out = [pltpu.make_async_copy(a, b, osem.at[9 + i]) for i, (a, b) in enumerate([(tv, o1), (fv, of), (gv, og)])]
    for x in loads + small_in:
        x.start()
    for i in range(9):
        loads[i].wait()
        wide[3 * i : 3 * i + 3] = narrow[3 * i : 3 * i + 3].astype(F32)
        stores[i].start()
    for a, b in zip(small_in, small_out):
        a.wait()
        b.start()
    for x in stores + small_out:
        x.wait()


def finish(gw, t, f, g):
    dma = pltpu.SemaphoreType.DMA
    return pl.pallas_call(
        finish_kernel,
        out_shape=[sds((27, 64, 1024), F32), sds((27, 64, 64), F32), sds((64, 1024)), sds((32, 2048))],
        in_specs=[ANY] * 4,
        out_specs=[ANY] * 4,
        scratch_shapes=[
            pltpu.VMEM((27, 64, 1024), BF16),
            pltpu.VMEM((27, 64, 1024), F32),
            pltpu.VMEM((27, 64, 64), F32),
            pltpu.VMEM((64, 1024), BF16),
            pltpu.VMEM((32, 2048), BF16),
            dma((12,)),
            dma((12,)),
        ],
        compiler_params=pltpu.CompilerParams(vmem_limit_bytes=16 * 1024 * 1024),
        name="finish",
    )(gw, t, f, g)


def on_device(volume, conv1_weight, conv2_weight, cotangent):
    feat, gvol, o1, gw = mega(volume.reshape(32, 2048), cotangent.reshape(64, 1024), conv1_weight, conv2_weight)
    o2, o1, feat, gvol = finish(gw, o1, feat, gvol)
    return feat.reshape(1, 1, 8, 8, 1024), gvol.reshape(1, 1, 32, 2048), o1, o2


def solution(mesh):
    return jax.shard_map(
        on_device,
        mesh=mesh,
        in_specs=(P("sample", "depth", None, None), P(), P(None, "depth", None), P("sample", "depth", None, None, None)),
        out_specs=(P("sample", "depth", None, None, None), P("sample", "depth", None, None), P(), P(None, "depth", None)),
        check_vma=False,
    )
```

```python
import functools
import math

import jax
import jax.numpy as jnp
from jax import lax
from jax.experimental import pallas as pl
from jax.experimental.pallas import tpu as pltpu
from jax.sharding import PartitionSpec as P

MESH = pl.DeviceIdType.MESH
F32 = jnp.float32
BF16 = jnp.bfloat16
ROOT = 0.7978845608028654
CUBIC = 0.044715
SCALE1 = 1.0 / math.sqrt(8 * 16 * 32 * 32)
SCALE2 = 1.0 / math.sqrt(8 * 16 * 8 * 8)
VM = pl.BlockSpec(memory_space=pltpu.VMEM)
ANY = pl.BlockSpec(memory_space=pl.ANY)
LIMIT = 60 * 1024 * 1024


def where_am_i():
    s = lax.axis_index("sample")
    d = lax.axis_index("depth")
    return s, d


def rcopy(src, dst, ss, rs, dev):
    return pltpu.make_async_remote_copy(
        src_ref=src, dst_ref=dst, send_sem=ss, recv_sem=rs, device_id=dev, device_id_type=MESH
    )


def depth_peer(d, jz, jy, jc):
    zh, y, c = d // 8, (d // 2) % 4, d % 2
    return ((zh + jz) % 2) * 8 + ((y + jy) % 4) * 2 + (c + jc) % 2


def depth_src(d, jz, jy, jc):
    zh, y, c = d // 8, (d // 2) % 4, d % 2
    return ((zh + jz) % 2) * 8 + ((y + 4 - jy) % 4) * 2 + (c + jc) % 2


def sample_peer(s, jz, jx):
    return ((s // 4 + jz) % 2) * 4 + (s % 4 + jx) % 4


def sample_src(s, jz, jx):
    return ((s // 4 + jz) % 2) * 4 + (s % 4 + 4 - jx) % 4


CHIPS = [(jz, jy) for jz in range(2) for jy in range(4) if (jz, jy) != (0, 0)]
SAMPS = [(jz, jx) for jz in range(2) for jx in range(4) if (jz, jx) != (0, 0)]


def barrier(devs):
    bar = pltpu.get_barrier_semaphore()
    for dev in devs:
        pl.semaphore_signal(bar, inc=1, device_id=dev, device_id_type=MESH)
    pl.semaphore_wait(bar, len(devs))


def onehot(shape, fn):
    row = lax.broadcasted_iota(jnp.int32, shape, 0)
    col = lax.broadcasted_iota(jnp.int32, shape, 1)
    return jnp.where(fn(row, col), 1.0, 0.0).astype(BF16)


def dot(a, b):
    return jnp.dot(a, b, preferred_element_type=F32)


def nat(rho):
    return 4 * (rho % 8) + rho // 8


def call(kern, outs, ins, scratch, name, cid=None, specs=None, out_specs=None, **kw):
    params = dict(vmem_limit_bytes=LIMIT)
    if cid is not None:
        params.update(collective_id=cid, has_side_effects=True)
    return pl.pallas_call(
        kern,
        out_shape=outs,
        in_specs=specs or [VM] * len(ins),
        out_specs=out_specs or [VM] * len(outs),
        scratch_shapes=scratch,
        compiler_params=pltpu.CompilerParams(**params),
        name=name,
    )(*ins)


def sds(shape, dtype=BF16):
    return jax.ShapeDtypeStruct(shape, dtype)


def depth_of(zh, y, c):
    return zh * 8 + y * 2 + c


def fill_rows(lhs, planes, perms):
    zero = jnp.zeros((32, 128), BF16)
    for a in range(3):
        for b in range(3):
            x = planes[a] if perms[b] is None else dot(perms[b], planes[a]).astype(BF16)
            xp = jnp.concatenate([zero, x, zero], axis=1)
            for j in range(8):
                lhs[pl.ds(j * 32, 32), pl.ds((3 * a + b) * 512, 512)] = xp[:, 256 * j : 256 * j + 512]


def edge_planes(prev, own, nxt, d):
    zero = jnp.zeros_like(own)
    return [jnp.where(d > 0, prev, zero), own, jnp.where(d < 15, nxt, zero)]


def gelu_parts(value):
    inner = ROOT * (value + CUBIC * value * value * value)
    return jnp.tanh(inner)


def row_shift(x, b):
    if b == 1:
        return x
    rows = x.shape[0]
    lane = lax.broadcasted_iota(jnp.int32, x.shape, 0) % 8
    if b == 0:
        return jnp.where(lane == 0, 0.0, pltpu.roll(x, 1, 0))
    return jnp.where(lane == 7, 0.0, pltpu.roll(x, rows - 1, 0))


def col_shift(x, c):
    if c == 1:
        return x
    zero = jnp.zeros((x.shape[0], 8, x.shape[2]), x.dtype)
    if c == 0:
        return jnp.concatenate([zero, x[:, :56]], axis=1)
    return jnp.concatenate([x[:, 8:], zero], axis=1)


def taps10(x, s2):
    n = x.shape[0]
    flat = x.astype(F32).reshape(n * 64, 128)
    for b in range(3):
        y = row_shift(flat, b).reshape(n, 64, 128)
        for c in range(3):
            s2[:, :, (3 * b + c) * 128 : (3 * b + c + 1) * 128] = col_shift(y, c).astype(BF16)


def put_band(band, ab, w3):
    zero = jnp.zeros((64, 64), BF16)
    left = jnp.concatenate([w3, zero], axis=0)
    right = jnp.concatenate([zero, w3], axis=0)
    both = jnp.concatenate([left, right], axis=1)
    band[pl.ds(ab * 512 + 64, 256), 0:128] = both
    band[pl.ds(ab * 512 + 192, 256), 128:256] = both


def fill_band(band, w1):
    band[...] = jnp.zeros_like(band)
    for ab in range(9):
        put_band(band, ab, w1[3 * ab : 3 * ab + 3].reshape(192, 64))


def fill_band_back(band, w1):
    band[...] = jnp.zeros_like(band)
    for ab in range(9):
        top = 3 * (8 - ab) + 2
        w3 = [jnp.transpose(w1[top - c].astype(F32)).astype(BF16) for c in range(3)]
        put_band(band, ab, jnp.concatenate(w3, axis=0))


STOP = None


class Done(Exception):
    pass


CHUNKS = [(4 * q, min(4, 27 - 4 * q)) for q in range(7)]
XF = (0, 1)
ZF = (2, 3, 4, 5, 6)


def mega_kernel(*refs):
    try:
        mega_body(*refs)
    except Done:
        pass


def mega_body(
    v, cot, w1, w,
    feat, gvol, o1, gw,
    vp, vn, cotp, mine, cb, csl, wv, mk, moved, lhs, lhsb, band, bandb, s2o, s2, part, zrecv, frecv,
    gm, grecv, acc, wacc, pre, ownf, psend, precv, gpn, gp, gn, tbuf, tall, rbuf, dbuf,
    wsem, hsem, asem, csem, xsem, msem, ssend, srecv, gsem, rsem, psem, nsend, nrecv, tsem,
):
    s, d = where_am_i()
    zh, y, c = d // 8, (d // 2) % 4, d % 2
    m = d // 2
    zl = s // 4
    up, down = (d + 1) % 16, (d + 15) % 16
    partner = depth_of(zh, y, 1 - c)
    yp, ym = depth_of(zh, (y + 1) % 4, c), depth_of(zh, (y + 3) % 4, c)
    late = []
    pend = {}

    def stop(k):
        if STOP == k:
            for fn in list(pend.values()):
                fn()
            for cond, cp in late:
                wait_late(cond, cp)
            raise Done

    def wait(k):
        pend.pop(k)()

    def wait_late(cond, cp):
        if cond is None:
            cp.wait_send()
        else:

            @pl.when(cond)
            def _():
                cp.wait_send()

    def go(src, dst, ss, rs, dev):
        cp = rcopy(src, dst, ss, rs, dev)
        cp.start()
        late.append((None, cp))

    def got(ref, ss, rs):
        rcopy(ref, ref, ss, rs, (s, partner)).wait_recv()

    def spread(src_of, dst, sems):
        k = d % 8
        for i, (jz, jy) in enumerate([(0, 0)] + CHIPS):
            t = depth_of((zh + jz) % 2, (y + jy) % 4, zh)
            if i:
                go(src_of(t // 2), dst(k + 1), sems.at[i], sems.at[16 + k], (s, t))
            else:
                cp = rcopy(src_of(t // 2), dst(k + 1), sems.at[i], sems.at[16 + k], (s, t))

                @pl.when(t != d)
                def _(cp=cp):
                    cp.start()

                late.append((t != d, cp))
        rim = (d == 7) | (d == 8)
        for i, (jz, jy) in enumerate(CHIPS):
            t = depth_of((zh + jz) % 2, (y + jy) % 4, 1 - zh)
            cp = rcopy(src_of(t // 2), dst(zh * 9), sems.at[8 + i], sems.at[24], (s, t))

            @pl.when(rim)
            def _(cp=cp):
                cp.start()

            late.append((rim, cp))

    def spread_wait(dst, sems):
        for k in range(8):

            @pl.when(8 * c + k != d)
            def _(k=k):
                got(dst(k + 1), sems.at[0], sems.at[16 + k])

        q = 9 - 9 * c

        @pl.when(8 - c != d)
        def _():
            got(dst(q), sems.at[0], sems.at[24])

    def home_send(src, buf, sems, edge):
        k = d % 8 + edge
        here, there = depth_of(zh, y, zh), depth_of(1 - zh, y, zh)
        go(src, buf.at[k], sems.at[1], sems.at[4 + c], (s, there))
        cp = rcopy(src, buf.at[k], sems.at[0], sems.at[4 + c], (s, here))

        @pl.when(c != zh)
        def _():
            cp.start()

        late.append((c != zh, cp))

        @pl.when(c == zh)
        def _():
            buf[k] = src[...]

    def home_wait(buf, sems, edge):
        for j in range(2):

            @pl.when((zh != c) | (c != j))
            def _(j=j):
                got(buf.at[2 * y + j + edge], sems.at[0], sems.at[4 + j])

    def ring_send(buf, sems, edge):
        two = buf.at[pl.ds(2 * y + edge, 2)]
        go(two, two, sems.at[2], sems.at[6], (s, yp))
        go(two, two, sems.at[3], sems.at[7], (s, ym))

    def ring_relay(buf, sems, edge):
        lo, hi = (y + 3) % 4, (y + 1) % 4
        got(buf.at[pl.ds(2 * lo + edge, 2)], sems.at[2], sems.at[6])
        one = buf.at[2 * lo + edge]
        go(one, one, sems.at[8], sems.at[10], (s, yp))
        got(buf.at[pl.ds(2 * hi + edge, 2)], sems.at[3], sems.at[7])
        one = buf.at[2 * hi + 1 + edge]
        go(one, one, sems.at[9], sems.at[11], (s, ym))

    def ring_wait(buf, sems, edge):
        far = (y + 2) % 4
        got(buf.at[2 * far + edge], sems.at[8], sems.at[10])
        got(buf.at[2 * far + 1 + edge], sems.at[9], sems.at[11])

    def features_z():
        cp = rcopy(part, zrecv, rsem.at[0], rsem.at[1], (s, depth_of(1 - zh, y, c)))

        @pl.when(zh != c)
        def _():
            cp.start()

        late.append((zh != c, cp))

    def features_y():
        cps = []
        for i in range(8):
            if i < 2:
                q, dev = 2 * y + i, depth_of(zh, y, i)
            else:
                q = 2 * ((y + i // 2) % 4) + i % 2
                dev = depth_of(zh, (y + i // 2) % 4, i % 2)
            cps.append((dev != d, rcopy(part.at[q], frecv.at[y], rsem.at[2 + i], rsem.at[10 + y], (s, dev))))

        @pl.when(zh == c)
        def _():
            got(zrecv, rsem.at[0], rsem.at[1])
            for i in range(8):
                part[i] = (part[i].astype(F32) + zrecv[i].astype(F32)).astype(BF16)
            for i, (cond, cp) in enumerate(cps):
                if i >= 2:
                    cp.start()
                else:

                    @pl.when(cond)
                    def _(cp=cp):
                        cp.start()

            frecv[y] = part[2 * y + c]

        for cond, cp in cps:
            late.append(((zh == c) & cond, cp))

    def features_wait():
        for j in range(4):

            @pl.when((j != y) | (zh != c))
            def _(j=j):
                got(frecv.at[j], rsem.at[0], rsem.at[10 + j])

    def to_owner(src, dst, sems, which=range(8)):
        for i in which:
            p = 8 * c + i
            cp = rcopy(src.at[i], dst.at[m], sems.at[i], sems.at[8 + m], (s, p))

            @pl.when(p != d)
            def _(cp=cp):
                cp.start()

            @pl.when(p == d)
            def _(i=i):
                dst[m] = src[i]

            late.append((p != d, cp))

    def owner_wait(dst, sems):
        for j in range(8):

            @pl.when(2 * j + zh != d)
            def _(j=j):
                got(dst.at[j], sems.at[0], sems.at[8 + j])

    xp, xm, x2 = sample_peer(s, 0, 1), sample_peer(s, 0, 3), sample_peer(s, 0, 2)
    zo, oxp, oxm, ox2 = sample_peer(s, 1, 0), sample_peer(s, 1, 1), sample_peer(s, 1, 3), sample_peer(s, 1, 2)

    class Gather:
        def __init__(self, ref, xf, zf, ss, rs):
            self.ref, self.xf, self.zf, self.ss, self.rs = ref, xf, zf, ss, rs

        def send(self, q, kind, block, dev):
            r = self.ref(block, q)
            go(r, r, self.ss.at[7 * q + kind], self.rs.at[7 * q + kind], (dev, d))

        def recv(self, q, kind, block):
            got(self.ref(block, q), self.ss.at[7 * q + kind], self.rs.at[7 * q + kind])

        def start(self, q):
            if q in self.zf:
                self.send(q, 0, s, zo)
            self.send(q, 1, s, xp)
            self.send(q, 2, s, xm)

        def start_z(self):
            for q in self.xf:
                self.send(q, 0, s, zo)

        def near(self, q):
            self.recv(q, 1, xm)
            if q % 2 == 0:
                self.send(q, 3, xm, xp)
            if q in self.xf:
                self.send(q, 4, xm, zo)
            self.recv(q, 2, xp)
            if q % 2:
                self.send(q, 3, xp, xm)
            if q in self.xf:
                self.send(q, 5, xp, zo)

        def across(self, q):
            self.recv(q, 0, zo)
            self.send(q, 4, zo, xp)
            self.send(q, 5, zo, xm)

        def far(self, q):
            self.recv(q, 3, x2)
            self.send(q, 6, x2, zo)

        def turn(self, q):
            self.recv(q, 4, oxm)
            if q % 2 == 0:
                self.send(q, 6, oxm, xp)
            self.recv(q, 5, oxp)
            if q % 2:
                self.send(q, 6, oxp, xm)

        def finish(self):
            for q in self.xf:
                self.recv(q, 0, zo)
                self.recv(q, 4, oxm)
                self.recv(q, 5, oxp)
                self.recv(q, 6, ox2)
            for q in self.zf:
                self.recv(q, 3, x2)
                self.recv(q, 6, ox2)

        def rest(self):
            for q in self.xf:
                self.near(q)
            for q in self.zf:
                self.across(q)
            for q in self.zf:
                self.near(q)
            for q in self.xf:
                self.far(q)
            for q in self.zf:
                self.turn(q)
            self.finish()

    agm = Gather(lambda b, q: mk.at[b, pl.ds(1 - c + 3 * q, 3)], (0,), (1, 2), ssend, srecv)
    agw = Gather(
        lambda b, q: gw.at[pl.ds(*CHUNKS[q]), :, pl.ds(pl.multiple_of(b * 128, 128), 128)], XF, ZF, nsend, nrecv
    )

    wl = pltpu.make_async_copy(w, wv.at[:, c], wsem.at[0])
    wl.start()
    pend["wl"] = wl.wait
    bar = pltpu.get_barrier_semaphore()
    friends = [
        (s, depth_peer(d, jz, jy, jc)) for jz in range(2) for jy in range(4) for jc in range(2) if (jz, jy, jc) != (0, 0, 0)
    ] + [(sample_peer(s, jz, jx), d) for jz, jx in SAMPS]
    for dev in friends:
        pl.semaphore_signal(bar, inc=1, device_id=dev, device_id_type=MESH)
    perm64 = onehot((64, 64), lambda u, q: q == (u % 8) * 8 + u // 8)
    cotp[...] = dot(perm64, cot[...]).astype(BF16)
    mine[s] = cotp[:, pl.ds(pl.multiple_of(s * 128, 128), 128)]
    cb[9 * c] = jnp.zeros((64, 1024), BF16)
    mk[:, 9 * c] = jnp.zeros((8, 64, 128), BF16)
    fill_band(band, w1)
    pl.semaphore_wait(bar, len(friends))
    stop(0)

    halo = [rcopy(v, vp, hsem.at[0], hsem.at[1], (s, up)), rcopy(v, vn, hsem.at[2], hsem.at[3], (s, down))]
    for h in halo:
        h.start()
    pend["halo"] = lambda: [h.wait() for h in halo]
    home_send(cotp, cb, csem, 1)
    for i, (jz, jx) in enumerate(SAMPS):
        t = sample_peer(s, jz, jx)
        go(cotp.at[:, pl.ds(pl.multiple_of(t * 128, 128), 128)], mine.at[s], asem.at[i], asem.at[7 + i], (t, d))
    wx = rcopy(w, wv.at[:, c], wsem.at[1], wsem.at[2], (s, partner))
    wx.start()
    pend["wx"] = wx.wait

    def mine_wait():
        for i, (jz, jx) in enumerate(SAMPS):
            got(mine.at[sample_src(s, jz, jx)], asem.at[i], asem.at[7 + i])

    pend["mine"] = mine_wait

    perms = [onehot((32, 32), lambda rho, i, b=b: i == nat(rho) + b - 1) for b in range(3)]
    wait("halo")
    fill_rows(lhs, edge_planes(vp[...], v[...], vn[...], d), perms)
    res = dot(lhs[...], band[...])
    for r in range(4):
        z = jnp.concatenate([res[j * 32 + r * 8 : j * 32 + r * 8 + 8] for j in range(8)], axis=0)
        pre[r] = z
        hid = (0.5 * z * (1.0 + gelu_parts(z))).astype(BF16)
        moved[2 * r] = hid[:, 0:128]
        moved[2 * r + 1] = hid[:, 128:256]
    spread(lambda t: moved.at[t], lambda k: mk.at[s, k], msem)
    pend["mk"] = lambda: spread_wait(lambda k: mk.at[s, k], msem)

    @pl.when(c == zh)
    def _():
        mk[s, d % 8 + 1] = moved[m]

    @pl.when((d == 7) | (d == 8))
    def _():
        mk[s, zh * 9] = moved[m]

    wait("mine")
    home_send(mine, csl, xsem, 0)
    fill_band_back(bandb, w1)
    wacc[...] = jnp.zeros_like(wacc)
    home_wait(csl, xsem, 0)
    ring_send(csl, xsem, 0)

    wait("mk")
    for q in range(3):
        agm.start(q)
    agm.start_z()
    if STOP == 1:
        pend["a"] = lambda: (ring_relay(csl, xsem, 0), home_wait(cb, csem, 1), ring_wait(csl, xsem, 0), agm.rest())
    stop(1)
    taps10(mk[s], s2o)
    wait("wl")
    wait("wx")

    def fwd(i):
        tot = jnp.zeros((256, 1024), F32)
        for a in range(3):
            tot = tot + dot(s2o[4 * i + a : 4 * i + a + 4].reshape(256, 1152), wv[9 * a : 9 * a + 9].reshape(1152, 1024))
        part[4 * i : 4 * i + 4] = tot.astype(BF16).reshape(4, 64, 1024)

    fwd(0)
    ring_relay(csl, xsem, 0)
    home_wait(cb, csem, 1)
    ring_send(cb, csem, 1)
    agm.near(0)
    agm.across(1)
    agm.across(2)
    fwd(1)
    agm.near(1)
    agm.near(2)
    agm.far(0)
    features_z()

    def fz():
        @pl.when(zh == c)
        def _():
            got(zrecv, rsem.at[0], rsem.at[1])

    pend["fz"] = fz
    ring_wait(csl, xsem, 0)

    def wpart(t, ref):
        ct = jnp.transpose(csl[:, t].reshape(512, 128).astype(F32)).astype(BF16)
        for a in range(3):
            wacc[:, 1152 * a : 1152 * a + 1152] += dot(ct, ref[a : a + 8].reshape(512, 1152))

    def wgrad(i, _):
        j = jnp.where(i == 2, 3, jnp.where(i == 3, 2, i))
        t = ((zl + j // 4) % 2) * 4 + (s % 4 + 4 - j % 4) % 4
        taps10(mk[t], s2)
        wpart(t, s2)
        return 0

    wpart(s, s2o)
    agm.turn(1)
    agm.turn(2)
    ring_relay(cb, csem, 1)
    lax.fori_loop(1, 3, wgrad, 0)
    if STOP == 2:
        pend["a"] = lambda: (agm.finish(), ring_wait(cb, csem, 1))
    stop(2)
    ring_wait(cb, csem, 1)
    go(cb.at[8 - 7 * c], cb.at[9 * c], csem.at[12], csem.at[13], (s, partner))
    agm.finish()
    lax.fori_loop(3, 5, wgrad, 0)
    got(cb.at[9 - 9 * c], csem.at[12], csem.at[13])
    stop(3)

    def back(i, _):
        tot = jnp.zeros((512, 384), F32)
        for a in range(3):
            rows = cb[2 - a : 10 - a].reshape(512, 1024)
            wt = wv[pl.ds(9 * a + 3 * i, 3)].reshape(384, 1024)
            tot = tot + lax.dot_general(rows, wt, (((1,), (1,)), ((), ())), preferred_element_type=F32)
        for j in range(3):
            acc[3 * i + j] = tot[:, 128 * j : 128 * j + 128]
        return 0

    lax.fori_loop(0, 3, back, 0)
    total = jnp.zeros((8, 64, 128), F32)
    for b in range(3):
        inner = jnp.zeros((8, 64, 128), F32)
        for cc in range(3):
            inner = inner + col_shift(acc[3 * b + cc].reshape(8, 64, 128), 2 - cc)
        total = total + row_shift(inner.reshape(512, 128), 2 - b).reshape(8, 64, 128)
    gm[...] = total.astype(BF16)
    to_owner(gm, grecv, gsem)
    pend["gm"] = lambda: owner_wait(grecv, gsem)
    lax.fori_loop(5, 8, wgrad, 0)
    stop(4)

    pcp = []
    for q, (lo, n) in enumerate(CHUNKS):
        for t in range(lo, lo + n):
            x = jnp.transpose(wacc[:, t * 128 : t * 128 + 128] * SCALE2)
            ownf[t] = jnp.where(c == 0, x[0:64], x[64:128])
            psend[t] = jnp.where(c == 0, x[64:128], x[0:64]).astype(BF16)
        cp = rcopy(psend.at[pl.ds(lo, n)], precv.at[pl.ds(lo, n)], psem.at[q], psem.at[7 + q], (s, partner))
        cp.start()
        pcp.append(cp)
    for q, (lo, n) in enumerate(CHUNKS):
        pcp[q].wait()
        gw[pl.ds(lo, n), :, pl.ds(pl.multiple_of(s * 128, 128), 128)] = (
            ownf[pl.ds(lo, n)] + precv[pl.ds(lo, n)].astype(F32)
        ).astype(BF16)
        agw.start(q)
    agw.start_z()
    if STOP == 5:
        agw.rest()
    stop(5)

    wait("gm")
    gpf = []
    for r in range(4):
        z = pre[r]
        th = gelu_parts(z)
        slope = 0.5 * (1.0 + th) + 0.5 * z * (1.0 - th * th) * ROOT * (1.0 + 3.0 * CUBIC * z * z)
        gpf.append(jnp.concatenate([grecv[2 * r], grecv[2 * r + 1]], axis=1).astype(F32) * slope)
    for j in range(8):
        rows = jnp.concatenate([gpf[r][8 * j : 8 * j + 8] for r in range(4)], axis=0)
        gpn[:, 256 * j : 256 * j + 256] = rows.astype(BF16)
    ghalo = [rcopy(gpn, gp, hsem.at[4], hsem.at[5], (s, up)), rcopy(gpn, gn, hsem.at[6], hsem.at[7], (s, down))]
    for h in ghalo:
        h.start()
    pend["ghalo"] = lambda: [h.wait() for h in ghalo]

    gx = jnp.concatenate([gpn[:, 256 * j : 256 * j + 256] for j in range(8)], axis=0)
    gt = jnp.transpose(gx.astype(F32)).astype(BF16)
    for ab in range(9):
        o = dot(gt, lhs[:, 512 * ab : 512 * ab + 512])
        even = o[0:64, 0:256] + o[128:192, 128:384]
        t = o[64:128, 128:384] + o[192:256, 256:512] + pltpu.roll(even, 192, 1)
        tbuf[64 * ab : 64 * ab + 64] = (t * SCALE1).astype(BF16)
    tbuf[576:640] = jnp.zeros((64, 256), BF16)

    offs = [(jz, jy, jc) for jz in range(2) for jy in range(4) for jc in range(2) if (jz, jy, jc) != (0, 0, 0)]

    def piece(t):
        return pl.ds(pl.multiple_of((t // 2) * 80, 16), 80), pl.ds(pl.multiple_of((t % 2) * 128, 128), 128)

    k2s = []
    for i, o in enumerate(offs):
        t = depth_peer(d, *o)
        k2s.append(rcopy(tbuf.at[piece(t)], rbuf.at[i], tsem.at[i], tsem.at[15 + i], (s, t)))
        k2s[-1].start()
    if STOP == 8:
        pend.pop("fz")
        for q in range(0):
            pass
        pend["fz"] = fz
    stop(8)
    pend.pop("fz")
    features_y()
    pend["part"] = features_wait
    for q in XF:
        agw.near(q)
    for q in ZF:
        agw.across(q)
    if STOP == 7:
        for q in ZF:
            agw.near(q)
        for q in XF:
            agw.far(q)
        for q in ZF:
            agw.turn(q)
        agw.finish()
        pend["k2"] = lambda: [x.wait() for x in k2s]
    stop(7)

    wait("ghalo")
    perms = [onehot((32, 32), lambda u, q, b=b: nat(q) == nat(u) + b - 1) for b in range(3)]
    perms[1] = None
    fill_rows(lhsb, edge_planes(gp[...], gpn[...], gn[...], d), perms)
    tot = tbuf[piece(d)].astype(F32)
    for i in range(15):
        k2s[i].wait()
        tot = tot + rbuf[i].astype(F32)
    dbuf[7] = tot.astype(BF16)
    k3s = []
    for i, (jz, jx) in enumerate(SAMPS):
        k3s.append(rcopy(dbuf.at[7], dbuf.at[i], tsem.at[30 + i], tsem.at[37 + i], (sample_peer(s, jz, jx), d)))
        k3s[-1].start()
    for q in ZF:
        agw.near(q)
    res = dot(lhsb[...], bandb[...]).astype(BF16)
    wide = jnp.concatenate([res[32 * j : 32 * j + 32] for j in range(8)], axis=1)
    gvol[...] = dot(onehot((32, 32), lambda i, q: nat(q) == i), wide).astype(BF16)
    for q in XF:
        agw.far(q)
    if STOP == 9:
        for q in ZF:
            agw.turn(q)
        agw.finish()
        pend["k3"] = lambda: [x.wait() for x in k3s]
    stop(9)
    wait("part")
    tot = frecv[0].astype(F32)
    for i in range(1, 4):
        tot = tot + frecv[i].astype(F32)
    feat[...] = dot(perm64, tot.astype(BF16)).astype(BF16)

    for q in ZF:
        agw.turn(q)
    for x in k3s:
        x.wait()
    tot = None
    for j in range(8):
        idx = ((j // 4 + zl) % 2) * 4 + (s % 4 + 4 - j % 4) % 4
        idx = jnp.where(idx == 0, 7, idx - 1)
        val = dbuf[idx].astype(F32)
        tot = val if tot is None else tot + val
    tall[piece(d)] = tot.astype(BF16)
    k4s = []
    for i, o in enumerate(offs):
        k4s.append(rcopy(tall.at[piece(d)], tall.at[piece(d)], tsem.at[44 + i], tsem.at[59 + i], (s, depth_peer(d, *o))))
        k4s[-1].start()

    for i, o in enumerate(offs):
        got(tall.at[piece(depth_src(d, *o))], tsem.at[44 + i], tsem.at[59 + i])
        k4s[i].wait_send()
    for ab in range(9):
        o1[3 * ab : 3 * ab + 3] = jnp.transpose(tall[64 * ab : 64 * ab + 64].astype(F32))[0:192].reshape(3, 64, 64)
    agw.finish()
    for cond, cp in late:
        wait_late(cond, cp)


def mega(v, cot, w1, w):
    dma = pltpu.SemaphoreType.DMA
    vm = lambda *shape: pltpu.VMEM(shape, BF16)
    vf = lambda *shape: pltpu.VMEM(shape, F32)
    scratch = [
        vm(32, 2048), vm(32, 2048), vm(64, 1024), vm(8, 64, 128), vm(10, 64, 1024), vm(8, 8, 64, 128),
        vm(27, 2, 64, 1024), vm(8, 10, 64, 128), vm(8, 64, 128), vm(256, 4608), vm(256, 4608), vm(4608, 256),
        vm(4608, 256), vm(10, 64, 1152), vm(10, 64, 1152), vm(8, 64, 1024), vm(8, 64, 1024), vm(4, 64, 1024),
        vm(8, 64, 128), vm(8, 64, 128), vf(9, 512, 128), vf(128, 3456), vf(4, 64, 256), vf(27, 64, 128),
        vm(27, 64, 128), vm(27, 64, 128), vm(32, 2048), vm(32, 2048), vm(32, 2048), vm(640, 256), vm(640, 256),
        vm(15, 80, 128), vm(8, 80, 128),
        dma((3,)), dma((8,)), dma((14,)), dma((14,)), dma((14,)), dma((25,)), dma((21,)), dma((21,)), dma((16,)), dma((16,)),
        dma((14,)), dma((49,)), dma((49,)), dma((74,)),
    ]
    return pl.pallas_call(
        mega_kernel,
        out_shape=[sds((64, 1024)), sds((32, 2048)), sds((27, 64, 64), F32), sds((27, 64, 1024))],
        in_specs=[VM, VM, VM, ANY],
        out_specs=[VM] * 4,
        scratch_shapes=scratch,
        compiler_params=pltpu.CompilerParams(vmem_limit_bytes=LIMIT, collective_id=1, has_side_effects=True),
        name="step",
    )(v, cot, w1, w)


def finish_kernel(gw, t, f, g, o2, o1, of, og, narrow, wide, tv, fv, gv, isem, osem):
    loads = [pltpu.make_async_copy(gw.at[pl.ds(3 * i, 3)], narrow.at[pl.ds(3 * i, 3)], isem.at[i]) for i in range(9)]
    small_in = [pltpu.make_async_copy(a, b, isem.at[9 + i]) for i, (a, b) in enumerate([(t, tv), (f, fv), (g, gv)])]
    stores = [pltpu.make_async_copy(wide.at[pl.ds(3 * i, 3)], o2.at[pl.ds(3 * i, 3)], osem.at[i]) for i in range(9)]
    small_out = [pltpu.make_async_copy(a, b, osem.at[9 + i]) for i, (a, b) in enumerate([(tv, o1), (fv, of), (gv, og)])]
    for x in loads + small_in:
        x.start()
    for i in range(9):
        loads[i].wait()
        wide[3 * i : 3 * i + 3] = narrow[3 * i : 3 * i + 3].astype(F32)
        stores[i].start()
    for a, b in zip(small_in, small_out):
        a.wait()
        b.start()
    for x in stores + small_out:
        x.wait()


def finish(gw, t, f, g):
    dma = pltpu.SemaphoreType.DMA
    return pl.pallas_call(
        finish_kernel,
        out_shape=[sds((27, 64, 1024), F32), sds((27, 64, 64), F32), sds((64, 1024)), sds((32, 2048))],
        in_specs=[ANY] * 4,
        out_specs=[ANY] * 4,
        scratch_shapes=[
            pltpu.VMEM((27, 64, 1024), BF16),
            pltpu.VMEM((27, 64, 1024), F32),
            pltpu.VMEM((27, 64, 64), F32),
            pltpu.VMEM((64, 1024), BF16),
            pltpu.VMEM((32, 2048), BF16),
            dma((12,)),
            dma((12,)),
        ],
        compiler_params=pltpu.CompilerParams(vmem_limit_bytes=LIMIT),
        name="finish",
    )(gw, t, f, g)


def on_device(volume, conv1_weight, conv2_weight, cotangent):
    feat, gvol, o1, gw = mega(volume.reshape(32, 2048), cotangent.reshape(64, 1024), conv1_weight, conv2_weight)
    o2, o1, feat, gvol = finish(gw, o1, feat, gvol)
    return feat.reshape(1, 1, 8, 8, 1024), gvol.reshape(1, 1, 32, 2048), o1, o2


def solution(mesh):
    return jax.shard_map(
        on_device,
        mesh=mesh,
        in_specs=(P("sample", "depth", None, None), P(), P(None, "depth", None), P("sample", "depth", None, None, None)),
        out_specs=(P("sample", "depth", None, None, None), P("sample", "depth", None, None), P(), P(None, "depth", None)),
        check_vma=False,
    )
```
